32 devices in a mesh: groups: 2 (over y), src: 4 (over z), tgt: 2 (over x), ill: 2 (over core).
Axes of the slice: x: 2, y: 2, z: 4, core: 2. Of those that a mesh axis runs over, the one named last changes fastest.
Arguments:
- coeffs: bfloat16 [2, 64, 8, 8, 512], P(None, ('groups', 'ill'), 'src', 'tgt'), parts along dimension 1, may hold values from -6 to 6
- reflection: float32 [2, 16, 8, 512], P(None, ('groups', 'src'), 'tgt'), parts along dimension 1, may hold values from -4.2 to 4.2
- interp: float32 [2, 3, 2, 2, 3, 8, 8], replicated, may hold values from -1 to 1
- orders: int32 [512], replicated, may hold values from 0 to 511, each once
Outputs:
- far_field: bfloat16 [2, 64, 8, 8, 512], P(None, ('groups', 'ill'), 'src', 'tgt'), parts along dimension 1
The draws below stay inside these ranges and needn't reach their ends.
There are 2 independent parts, one for each index of `groups`. The reference program is written for one: setup_inputs(seed, part) draws one part's arguments, and reference() takes and returns one part's arrays. A program takes and returns all parts, laid end to end along the dimension named above; an argument that names none is the same for every part. Nothing has to cross between parts.
Inputs may be any that keep to these rules, and one draw needn't show every extreme that they name: `orders`: each number below 512 appears exactly once.
All inputs are finite; a program needn't handle non-finite values.
Results may differ from the reference program's by a relative error of at most 0.028.
Values may be sent and summed in bfloat16 or wider, within the bound.
A program may use at most 64 MiB of HBM per device.

```python
import math
import jax
import jax.numpy as jnp
from jax import lax

ORDER = 8
K = 512
LEVELS = 3
ILLUM = 32
NU = 8
NV = 8


factor_scale = 0.8908987181403393


def draw_interp(key, part):
    matrix_count = 2 * LEVELS * 2 * 2 * 3
    vectors = jax.random.normal(key, (matrix_count, ORDER, ORDER), jnp.float32)
    identity = jnp.eye(ORDER, dtype=jnp.float32)
    result = jnp.broadcast_to(identity, (matrix_count, ORDER, ORDER))
    for turn_index in range(ORDER):
        column = vectors[:, turn_index, :]
        lengths = jnp.sum(column * column, axis=-1) + 1e-06
        reflector = identity[None, :, :] - 2.0 * column[:, :, None] * column[:, None, :] / lengths[:, None, None]
        result = jnp.einsum('nij,njk->nik', result, reflector, precision=lax.Precision.HIGHEST)
    result = result * factor_scale
    return result.reshape(2, LEVELS, 2, 2, 3, ORDER, ORDER).astype(jnp.float32)


def level_of(stream_key, shape, split, smallest, top_value):
    loudness, own = 1.0, jax.random.fold_in(stream_key, 6)
    for dim, blocks in split:
        steps = jnp.exp(jax.random.uniform(jax.random.fold_in(own, dim), (blocks,), jnp.float32, smallest / len(split), top_value / len(split)))
        loudness = loudness * jnp.repeat(steps, shape[dim] // blocks).reshape([-1 if axis == dim else 1 for axis in range(len(shape))])
    return loudness


def scatter_about(key, shape, deviation, most, cuts=(), held_as=jnp.bfloat16):
    entries = deviation * jax.random.normal(key, shape, jnp.float32)
    if cuts:
        entries = entries * level_of(key, shape, cuts, -0.22, 0.18)
    return jnp.clip(entries, -most, most).astype(held_as)


def setup_inputs(seed: int = 0, part: int = 0) -> dict:
    key_of = jax.random.split(jax.random.key(seed), 5)
    part_keys = jax.random.split(jax.random.fold_in(key_of[4], part), 5)
    return {
        "coeffs": scatter_about(part_keys[0], (2, ILLUM, NU, NV, K), 1.0, 6.0, ((1, 2), (2, 4), (3, 2))),
        "reflection": scatter_about(part_keys[1], (2, NU, NV, K), 0.7, 4.2, ((1, 4), (2, 2)), jnp.float32),
        "interp": draw_interp(jax.random.fold_in(key_of[4], 71), part),
        "orders": jax.random.permutation(key_of[3], K).astype(jnp.int32),
    }


PHASE_RATE = 0.3
ALONG_SECOND = 1.7
DIRECTIONS = ((0.6, 0.48, 0.64), (-0.36, 0.8, 0.48))


def node_value(digits, order_count):
    return jnp.cos(math.pi * (2.0 * digits.astype(jnp.float32) + 1.0) / (2.0 * order_count))


def node_products(orders, operator_index, order_count):
    square = order_count * order_count
    digit_first = orders // square
    digit_second = (orders // order_count) % order_count
    digit_third = orders % order_count
    direction = DIRECTIONS[operator_index]
    summed = direction[0] * node_value(digit_first, order_count)
    summed = summed + direction[1] * node_value(digit_second, order_count)
    return summed + direction[2] * node_value(digit_third, order_count)


def phase_table(products, level_index, u_positions, v_positions):
    position = (u_positions[:, None] + 0.5) + ALONG_SECOND * (v_positions[None, :] + 0.5)
    angle_table = (PHASE_RATE * (level_index + 1)) * position[:, :, None] * products[None, None, :]
    return jnp.cos(angle_table).astype(jnp.bfloat16), jnp.sin(angle_table).astype(jnp.bfloat16)


def modulate(current, cos_part, sin_part):
    real_part = current[0].astype(jnp.float32)
    imag_part = current[1].astype(jnp.float32)
    cos_value = cos_part.astype(jnp.float32)
    sin_value = sin_part.astype(jnp.float32)
    return jnp.stack([cos_value * real_part - sin_value * imag_part,
                      cos_value * imag_part + sin_value * real_part]).astype(jnp.bfloat16)


def reflect(current, reflection):
    real_part = current[0].astype(jnp.float32)
    imag_part = current[1].astype(jnp.float32)
    return jnp.stack([reflection[0] * real_part - reflection[1] * imag_part,
                      reflection[0] * imag_part + reflection[1] * real_part]).astype(jnp.bfloat16)


def dense_transposed(factors):
    order_count = factors.shape[-1]
    coef_count = order_count ** 3
    columns = jnp.arange(coef_count, dtype=jnp.int32)
    digit_list = (columns // (order_count * order_count), (columns // order_count) % order_count,
                  columns % order_count)
    point_index = jnp.arange(order_count, dtype=jnp.int32)
    spread = []
    for dim_index in range(3):
        selector = (point_index[:, None] == digit_list[dim_index][None, :]).astype(factors.dtype)
        spread.append(jnp.dot(factors[dim_index].T, selector, precision=lax.Precision.HIGHEST))
    full_table = spread[0][:, None, None, :] * spread[1][None, :, None, :]
    full_table = full_table * spread[2][None, None, :, :]
    return full_table.reshape(coef_count, coef_count).astype(jnp.bfloat16)


def pair_level(current, products, factors, level_index, box_axis, pair_bit, u_positions, v_positions):
    cos_part, sin_part = phase_table(products, level_index, u_positions, v_positions)
    modulated = modulate(current, cos_part, sin_part)
    full_shape = modulated.shape
    coef_count = full_shape[-1]
    half_span = 2 ** pair_bit
    split_shape = full_shape[:box_axis] + (full_shape[box_axis] // (2 * half_span), 2, half_span) + full_shape[box_axis + 1:]
    halves = modulated.reshape(split_shape)
    lower_half = jnp.take(halves, 0, axis=box_axis + 1)
    upper_half = jnp.take(halves, 1, axis=box_axis + 1)
    outputs = []
    for side_index in range(2):
        lower_matrix = dense_transposed(factors[side_index, 0])
        upper_matrix = dense_transposed(factors[side_index, 1])
        summed = jnp.dot(lower_half.reshape(-1, coef_count), lower_matrix, preferred_element_type=jnp.float32)
        summed = summed + jnp.dot(upper_half.reshape(-1, coef_count), upper_matrix, preferred_element_type=jnp.float32)
        outputs.append(summed.reshape(lower_half.shape))
    combined = jnp.stack(outputs, axis=box_axis + 1).reshape(full_shape)
    return combined.astype(jnp.bfloat16)


def reference(coeffs, reflection, interp, orders):
    order_count = interp.shape[-1]
    u_positions = jnp.arange(NU, dtype=jnp.int32).astype(jnp.float32)
    v_positions = jnp.arange(NV, dtype=jnp.int32).astype(jnp.float32)
    current = coeffs
    for operator_index, box_axis, extent in ((0, 2, NU), (1, 3, NV)):
        products = node_products(orders, operator_index, order_count)
        top_bit = extent.bit_length() - 2
        for level_index in range(LEVELS):
            current = pair_level(current, products, interp[operator_index, level_index], level_index,
                                 box_axis, top_bit - level_index, u_positions, v_positions)
        if operator_index == 0:
            current = reflect(current, reflection)
    return current
```

```python
import functools
import math

import jax
import jax.numpy as jnp
from jax import lax
from jax.experimental import pallas as pl
from jax.experimental.pallas import tpu as pltpu
from jax.sharding import PartitionSpec as P

PHASE_RATE = 0.3
ALONG_SECOND = 1.7
DIRECTIONS = ((0.6, 0.48, 0.64), (-0.36, 0.8, 0.48))
SHARES = (2, 4, 5, 5)
LEAD = 3
LAG = 2
MESH = pl.DeviceIdType.MESH


def level_plan(level_count, boxes, sizes):
    plan = []
    for operator, axis in enumerate(("src", "tgt")):
        local_bits = boxes[operator].bit_length() - 1
        top_bit = (boxes[operator] * sizes[operator]).bit_length() - 2
        row_span = boxes[1] if operator == 0 else 1
        for level in range(level_count):
            bit = top_bit - level
            if bit >= local_bits:
                plan.append((operator, level, axis, 2 ** (bit - local_bits)))
            else:
                plan.append((operator, level, None, row_span * 2**bit))
    return plan


def own_bit(axis, mask):
    return lax.rem(lax.div(lax.axis_index(axis), mask), 2)


def partner_of(axis, mask):
    return lax.axis_index(axis) + mask * (1 - 2 * own_bit(axis, mask))


def swap_kernel(
    plan,
    boxes,
    sizes,
    coeffs,
    reflection_far,
    interp_far,
    orders_far,
    out,
    own,
    reflection,
    interp,
    orders,
    landed,
    held,
    sent,
    total,
    rows,
    spread,
    phase,
    weight,
    mirror,
    own_sem,
    send_sem,
    recv_sem,
):
    order_count = interp.shape[-1]
    coef_count = coeffs.shape[-1]
    first, second = boxes
    tile = first * second
    chunks = len(sizes)
    starts = [sum(sizes[:c]) for c in range(chunks)]
    swaps = [n for n, item in enumerate(plan) if item[2] is not None]

    def chunk(c):
        return pl.ds(2 * tile * starts[c], 2 * tile * sizes[c])

    barrier = pltpu.get_barrier_semaphore()
    for n in swaps:
        axis, mask = plan[n][2:]
        pl.semaphore_signal(
            barrier, inc=1, device_id={axis: partner_of(axis, mask)}, device_id_type=MESH
        )
    pl.semaphore_wait(barrier, len(swaps))

    def raw_copy(c):
        axis, mask = plan[0][2:]
        return pltpu.make_async_remote_copy(
            src_ref=coeffs.at[:, pl.ds(starts[c], sizes[c])],
            dst_ref=landed.at[:, pl.ds(starts[c], sizes[c])],
            send_sem=send_sem.at[0, c],
            recv_sem=recv_sem.at[0, c],
            device_id={axis: partner_of(axis, mask)},
            device_id_type=MESH,
        )

    def state_copy(s, c):
        axis, mask = plan[swaps[s]][2:]
        return pltpu.make_async_remote_copy(
            src_ref=sent.at[s - 1, chunk(c)],
            dst_ref=held.at[s - 1, chunk(c)],
            send_sem=send_sem.at[s, c],
            recv_sem=recv_sem.at[s, c],
            device_id={axis: partner_of(axis, mask)},
            device_id_type=MESH,
        )

    lead = min(LEAD, chunks) if len(swaps) > 1 else chunks
    for c in range(lead):
        raw_copy(c).start()
    own_copy = pltpu.make_async_copy(coeffs, own, own_sem.at[0])
    near = [
        pltpu.make_async_copy(orders_far, orders, own_sem.at[1]),
        pltpu.make_async_copy(interp_far, interp, own_sem.at[2]),
        pltpu.make_async_copy(reflection_far, reflection, own_sem.at[3]),
    ]
    for copy in near:
        copy.start()
    own_copy.start()
    near[0].wait()

    digits = (
        lax.div(orders[...], order_count * order_count),
        lax.rem(lax.div(orders[...], order_count), order_count),
        lax.rem(orders[...], order_count),
    )
    values = [
        jnp.cos(math.pi * (2.0 * d.astype(jnp.float32) + 1.0) / (2.0 * order_count))
        for d in digits
    ]
    products = []
    for direction in DIRECTIONS:
        summed = direction[0] * values[0] + direction[1] * values[1]
        products.append(summed + direction[2] * values[2])
    row = lax.broadcasted_iota(jnp.int32, (tile, coef_count), 0)

    def fill_phase(slot, operator, level, u_start, v_start):
        u = (lax.div(row, second) + u_start).astype(jnp.float32)
        v = (lax.rem(row, second) + v_start).astype(jnp.float32)
        position = (u + 0.5) + ALONG_SECOND * (v + 0.5)
        angle = (PHASE_RATE * (level + 1)) * position * products[operator]
        phase[slot, 0] = jnp.cos(angle).astype(jnp.bfloat16).astype(jnp.float32)
        phase[slot, 1] = jnp.sin(angle).astype(jnp.bfloat16).astype(jnp.float32)

    u_own = lax.axis_index("src") * first
    v_own = lax.axis_index("tgt") * second
    fill_phase(0, plan[0][0], plan[0][1], u_own, v_own)

    column = lax.broadcasted_iota(jnp.int32, (order_count, coef_count), 1)
    point = lax.broadcasted_iota(jnp.int32, (order_count, coef_count), 0)
    column_digits = (
        lax.div(column, order_count * order_count),
        lax.rem(lax.div(column, order_count), order_count),
        lax.rem(column, order_count),
    )
    near[1].wait()
    for d in range(3):
        selector = (point == column_digits[d]).astype(jnp.float32)
        factors = interp[:, :, :, :, d].reshape(-1, order_count, order_count)
        factors = jnp.swapaxes(factors, 1, 2).reshape(-1, order_count)
        spread[d] = jnp.dot(
            factors, selector, precision=lax.Precision.HIGHEST,
            preferred_element_type=jnp.float32,
        )

    square = order_count * order_count

    def build(slot, index):
        where = pl.ds(pl.multiple_of(index * order_count, order_count), order_count)
        first_factor = spread[0, where, :]
        second_factor = spread[1, where, :]
        third_factor = spread[2, where, :]
        for a in range(order_count):
            pair = first_factor[a : a + 1, :] * second_factor
            block = pair[:, None, :] * third_factor[None, :, :]
            weight[slot, pl.ds(a * square, square), :] = block.reshape(
                square, coef_count
            ).astype(jnp.bfloat16)

    level_count = interp.shape[1]
    slots = []
    used = 0
    for item in plan:
        slots.append(used)
        used += 2 if item[2] is not None else 4

    def build_level(n):
        operator, level, axis, mask = plan[n]
        base = (operator * level_count + level) * 4
        if axis is None:
            def step(j, carry):
                build(slots[n] + j, base + j)
                return carry
            lax.fori_loop(0, 4, step, 0)
        else:
            bit = own_bit(axis, mask)

            def step(j, carry):
                child = bit + j - 2 * bit * j
                build(slots[n] + j, base + 2 * bit + child)
                return carry
            lax.fori_loop(0, 2, step, 0)

    def dot(left, slot):
        return jnp.dot(left, weight[slot], preferred_element_type=jnp.float32)

    def modulate(value, cos_part, sin_part):
        half = value.shape[0] // 2
        shape = (half // tile, tile, coef_count)
        real = value[:half].reshape(shape)
        imag = value[half:].reshape(shape)
        new_real = cos_part * real - sin_part * imag
        new_imag = cos_part * imag + sin_part * real
        return jnp.concatenate(
            [new_real.reshape(half, coef_count), new_imag.reshape(half, coef_count)], axis=0
        ).astype(jnp.bfloat16)

    def gather_rows(ref, c):
        for p in range(2):
            for i in range(sizes[c]):
                for u in range(first):
                    at = (p * sizes[c] + i) * tile + u * second
                    rows[pl.ds(at, second), :] = ref[p, starts[c] + i, u].astype(jnp.float32)
        return rows[: 2 * sizes[c] * tile, :]

    build_level(0)
    own_copy.wait()

    for c in range(chunks):
        moved = modulate(gather_rows(own, c), phase[0, 0], phase[0, 1])
        total[0, chunk(c), :] = dot(moved, slots[0])

    axis, mask = plan[0][2:]
    shift = (partner_of(axis, mask) - lax.axis_index(axis)) * (
        first if axis == "src" else second
    )
    fill_phase(
        len(plan),
        plan[0][0],
        plan[0][1],
        u_own + (shift if axis == "src" else 0),
        v_own + (shift if axis == "tgt" else 0),
    )
    ends = [0] + swaps[1:] + [len(plan) - 1]

    def prepare(s):
        for n in range(ends[s] + 1, ends[s + 1] + 1):
            fill_phase(n, plan[n][0], plan[n][1], u_own, v_own)
            build_level(n)

    prepare(0)
    near[2].wait()
    for p in range(2):
        for u in range(first):
            mirror[p, pl.ds(u * second, second), :] = reflection[p, u]

    def stage(s, c):
        n = swaps[s]
        if s == 0:
            raw_copy(c).wait_recv()
            value = gather_rows(landed, c)
            received = modulate(value, phase[len(plan), 0], phase[len(plan), 1])
        else:
            state_copy(s, c).wait_recv()
            received = held[s - 1, chunk(c), :]
        chunk_rows = 2 * tile * sizes[c]
        row_index = lax.broadcasted_iota(jnp.int32, (chunk_rows, coef_count), 0)
        summed = total[s, chunk(c), :] + dot(received, slots[n] + 1)
        state = summed.astype(jnp.bfloat16).astype(jnp.float32)
        last = swaps[s + 1] if s + 1 < len(swaps) else len(plan)
        for m in range(n + 1, last + 1):
            before = plan[m - 1][0]
            if before == 0 and (m == len(plan) or plan[m][0] == 1):
                state = (
                    modulate(state, mirror[0], mirror[1]).astype(jnp.float32)
                )
            if m == len(plan):
                break
            moved = modulate(state, phase[m, 0], phase[m, 1])
            if m == last:
                sent[s, chunk(c), :] = moved
                state_copy(s + 1, c).start()
                if s == 0 and c + lead < chunks:
                    raw_copy(c + lead).start()
                total[s + 1, chunk(c), :] = dot(moved, slots[m])
                return
            span = plan[m][3]
            upper_row = lax.rem(lax.div(row_index, span), 2) == 1
            wide = moved.astype(jnp.float32)
            lower = jnp.where(upper_row, pltpu.roll(wide, span, 0), wide).astype(jnp.bfloat16)
            upper = jnp.where(
                upper_row, wide, pltpu.roll(wide, chunk_rows - span, 0)
            ).astype(jnp.bfloat16)
            low = dot(lower, slots[m]) + dot(upper, slots[m] + 1)
            high = dot(lower, slots[m] + 2) + dot(upper, slots[m] + 3)
            state = jnp.where(upper_row, high, low).astype(jnp.bfloat16).astype(jnp.float32)
        result = state.astype(jnp.bfloat16).reshape(2, sizes[c], tile, coef_count)
        out[:, pl.ds(starts[c], sizes[c])] = result

    for t in range(chunks + LAG * (len(swaps) - 1)):
        for s in range(len(swaps)):
            if 0 <= t - LAG * s < chunks:
                stage(s, t - LAG * s)
        if 1 <= t + 1 < len(swaps):
            prepare(t + 1)

    for c in range(chunks):
        raw_copy(c).wait_send()
        for s in range(1, len(swaps)):
            state_copy(s, c).wait_send()


def by_swaps(coeffs, reflection, interp, orders):
    level_count = interp.shape[1]
    order_count = interp.shape[-1]
    _, ills, first, second, coef_count = coeffs.shape
    sizes_of = [ills * share // sum(SHARES) for share in SHARES]
    sizes_of[0] += ills - sum(sizes_of)
    sizes_of = [size for size in sizes_of if size > 0]
    chunks = len(sizes_of)
    tile = first * second
    sizes = (lax.axis_size("src"), lax.axis_size("tgt"))
    plan = level_plan(level_count, (first, second), sizes)
    swap_count = sum(item[2] is not None for item in plan)
    slot_count = 2 * swap_count + 4 * (len(plan) - swap_count)
    state_rows = 2 * ills * tile
    later = max(swap_count - 1, 1)
    whole = pl.BlockSpec(memory_space=pltpu.VMEM)
    result = pl.pallas_call(
        functools.partial(swap_kernel, plan, (first, second), sizes_of),
        out_shape=jax.ShapeDtypeStruct((2, ills, tile, coef_count), jnp.bfloat16),
        in_specs=[pl.BlockSpec(memory_space=pl.ANY)] * 4,
        out_specs=whole,
        scratch_shapes=[
            pltpu.VMEM(coeffs.shape, jnp.bfloat16),
            pltpu.VMEM(reflection.shape, jnp.float32),
            pltpu.VMEM(interp.shape, jnp.float32),
            pltpu.VMEM((1, coef_count), jnp.int32),
            pltpu.VMEM(coeffs.shape, jnp.bfloat16),
            pltpu.VMEM((later, state_rows, coef_count), jnp.bfloat16),
            pltpu.VMEM((later, state_rows, coef_count), jnp.bfloat16),
            pltpu.VMEM((swap_count, state_rows, coef_count), jnp.float32),
            pltpu.VMEM((2 * tile * max(sizes_of), coef_count), jnp.float32),
            pltpu.VMEM((3, 8 * level_count * order_count, coef_count), jnp.float32),
            pltpu.VMEM((len(plan) + 1, 2, tile, coef_count), jnp.float32),
            pltpu.VMEM((slot_count, coef_count, coef_count), jnp.bfloat16),
            pltpu.VMEM((2, tile, coef_count), jnp.float32),
            pltpu.SemaphoreType.DMA((4,)),
            pltpu.SemaphoreType.DMA((swap_count, chunks)),
            pltpu.SemaphoreType.DMA((swap_count, chunks)),
        ],
        compiler_params=pltpu.CompilerParams(
            collective_id=0, has_side_effects=True, vmem_limit_bytes=60 * 2**20
        ),
        name="butterfly",
    )(coeffs, reflection, interp, orders.reshape(1, coef_count))
    return result.reshape(coeffs.shape)


def flipped(axis, mask):
    index = lax.axis_index(axis)
    for bit in range(mask.bit_length()):
        if mask >> bit & 1:
            index = index + 2**bit * (1 - 2 * lax.rem(lax.div(index, 2**bit), 2))
    return index


def spread_kernel(
    spans,
    coeffs,
    reflection_far,
    interp_far,
    orders_far,
    out,
    reflection,
    interp,
    orders,
    landed,
    back,
    mirror_out,
    mirror_in,
    rows,
    spread,
    phase,
    mirror,
    weight,
    near_sem,
    send_sem,
    recv_sem,
    back_send_sem,
    back_recv_sem,
    mirror_send_sem,
    mirror_recv_sem,
):
    src_span, tgt_span = spans
    chunks = landed.shape[0]
    order_count = interp.shape[-1]
    level_count = interp.shape[1]
    coef_count = coeffs.shape[-1]
    first, second = coeffs.shape[2:4]
    u_count, v_count = src_span * first, tgt_span * second
    box_count = u_count * v_count
    square = order_count * order_count

    u_home = lax.axis_index("src")
    v_home = lax.axis_index("tgt")
    core = lax.axis_index("ill")
    home = u_home * tgt_span + v_home
    offsets = [(du, dv) for du in reversed(range(src_span)) for dv in reversed(range(tgt_span))]

    def device(k):
        return {
            "src": flipped("src", offsets[k][0]),
            "tgt": flipped("tgt", offsets[k][1]),
            "ill": 1 - core,
        }

    def place(k):
        return flipped("src", offsets[k][0]) * tgt_span + flipped("tgt", offsets[k][1])

    barrier = pltpu.get_barrier_semaphore()
    for k in range(len(offsets)):
        pl.semaphore_signal(barrier, inc=1, device_id=device(k), device_id_type=MESH)

    near = [
        pltpu.make_async_copy(orders_far, orders, near_sem.at[0]),
        pltpu.make_async_copy(reflection_far, reflection, near_sem.at[1]),
        pltpu.make_async_copy(interp_far, interp, near_sem.at[2]),
    ]
    for copy in near:
        copy.start()

    def out_copy(c, k):
        return pltpu.make_async_remote_copy(
            src_ref=coeffs.at[:, pl.ds(place(k) * chunks + c, 1)],
            dst_ref=landed.at[c, home],
            send_sem=send_sem.at[c, k],
            recv_sem=recv_sem.at[c, k],
            device_id=device(k),
            device_id_type=MESH,
        )

    def back_copy(c, k):
        return pltpu.make_async_remote_copy(
            src_ref=back.at[c, place(k)],
            dst_ref=out.at[:, pl.ds(home * chunks + c, 1)],
            send_sem=back_send_sem.at[c, k],
            recv_sem=back_recv_sem.at[c, k],
            device_id=device(k),
            device_id_type=MESH,
        )

    def mirror_copy(k):
        if offsets[k] == (0, 0):
            source, target = mirror_in.at[1 - core], mirror_in.at[1 - core]
        else:
            source, target = mirror_out.at[core], mirror_in.at[core, home]
        return pltpu.make_async_remote_copy(
            src_ref=source,
            dst_ref=target,
            send_sem=mirror_send_sem.at[k],
            recv_sem=mirror_recv_sem.at[k],
            device_id=device(k),
            device_id_type=MESH,
        )

    near[1].wait()
    mirror_out[...] = reflection[...].astype(jnp.bfloat16)
    mirror_in[1 - core, home] = mirror_out[1 - core]

    pl.semaphore_wait(barrier, len(offsets))
    for k in range(len(offsets)):
        out_copy(0, k).start()
    for k in range(len(offsets) - 1):
        mirror_copy(k).start()
    for c in range(1, chunks):
        for k in range(len(offsets)):
            out_copy(c, k).start()

    near[0].wait()
    digits = (
        lax.div(orders[...], square),
        lax.rem(lax.div(orders[...], order_count), order_count),
        lax.rem(orders[...], order_count),
    )
    values = [
        jnp.cos(math.pi * (2.0 * d.astype(jnp.float32) + 1.0) / (2.0 * order_count))
        for d in digits
    ]

    def times(left, right):
        return (
            left[0] * right[0] - left[1] * right[1],
            left[0] * right[1] + left[1] * right[0],
        )

    def fill_phases(operator):
        direction = DIRECTIONS[operator]
        node = direction[0] * values[0] + direction[1] * values[1]
        node = node + direction[2] * values[2]
        turns = []
        for count, rate in ((u_count, PHASE_RATE), (v_count, PHASE_RATE * ALONG_SECOND)):
            position = lax.broadcasted_iota(jnp.int32, (count, coef_count), 0)
            angle = rate * (position.astype(jnp.float32) + 0.5) * node
            turns.append((jnp.cos(angle), jnp.sin(angle)))
        u_turn, v_turn = turns
        u_now, v_now = u_turn, v_turn
        for level in range(level_count):
            if level:
                u_now, v_now = times(u_now, u_turn), times(v_now, v_turn)
            n = operator * level_count + level
            outer, inner = (u_now, v_now) if n <= level_count else (v_now, u_now)
            span = inner[0].shape[0]
            for i in range(outer[0].shape[0]):
                turn = times((outer[0][i : i + 1], outer[1][i : i + 1]), inner)
                phase[n, 0, pl.ds(i * span, span), :] = turn[0]
                phase[n, 1, pl.ds(i * span, span), :] = turn[1]

    for operator in range(2):
        fill_phases(operator)

    column = lax.broadcasted_iota(jnp.int32, (order_count, coef_count), 1)
    point = lax.broadcasted_iota(jnp.int32, (order_count, coef_count), 0)
    column_digits = (
        lax.div(column, square),
        lax.rem(lax.div(column, order_count), order_count),
        lax.rem(column, order_count),
    )
    near[2].wait()
    for d in range(3):
        selector = (point == column_digits[d]).astype(jnp.float32)
        factors = interp[:, :, :, :, d].reshape(-1, order_count, order_count)
        factors = jnp.swapaxes(factors, 1, 2).reshape(-1, order_count)
        spread[d] = jnp.dot(
            factors, selector, precision=lax.Precision.HIGHEST,
            preferred_element_type=jnp.float32,
        )

    def build(index, carry):
        where = pl.ds(pl.multiple_of(index * order_count, order_count), order_count)
        n = lax.div(index, 4)
        side = lax.rem(lax.div(index, 2), 2)
        child = lax.rem(index, 2)
        columns = pl.ds(pl.multiple_of(side * coef_count, coef_count), coef_count)
        first_factor = spread[0, where, :]
        second_factor = spread[1, where, :]
        third_factor = spread[2, where, :]
        for a in range(order_count):
            pair = first_factor[a : a + 1, :] * second_factor
            block = pair[:, None, :] * third_factor[None, :, :]
            at = pl.multiple_of(child * coef_count + a * square, square)
            weight[n, pl.ds(at, square), columns] = block.reshape(square, coef_count).astype(
                jnp.bfloat16
            )
        return carry

    lax.fori_loop(0, 4 * 2 * level_count, build, 0)

    for k in range(len(offsets) - 1):
        mirror_copy(k).wait_recv()
    mirror_copy(len(offsets) - 1).start()

    def modulate(blocks, table, n):
        result = [[], []]
        for i, (real, imag) in enumerate(zip(*blocks)):
            span = real.shape[0]
            at = pl.ds(i * span, span)
            new = times((table[n, 0, at, :], table[n, 1, at, :]), (real, imag))
            result[0].append(new[0])
            result[1].append(new[1])
        return result

    def apply_level(blocks, n, bit):
        count = len(blocks[0])
        low = [i for i in range(count) if not i >> bit & 1]
        parts = [
            jnp.concatenate([blocks[p][i + side * 2**bit] for p in range(2) for i in low], axis=0)
            for side in range(2)
        ]
        left = jnp.concatenate(parts, axis=1).astype(jnp.bfloat16)
        result = jnp.dot(left, weight[n], preferred_element_type=jnp.float32)
        new = [[None] * count, [None] * count]
        span = blocks[0][0].shape[0]
        for p in range(2):
            for at, i in enumerate(low):
                start = (p * len(low) + at) * span
                for side in range(2):
                    new[p][i + side * 2**bit] = result[
                        start : start + span, side * coef_count : (side + 1) * coef_count
                    ]
        return new

    def place_blocks(blocks):
        for p in range(2):
            for i, block in enumerate(blocks[p]):
                span = block.shape[0]
                lanes = rows.shape[-1]
                for g in range(rows.shape[0]):
                    rows[g, pl.ds(p * box_count + i * span, span), :] = block[
                        :, g * lanes : (g + 1) * lanes
                    ]

    def take(start, count, stride):
        return jnp.concatenate(
            [rows[g, pl.ds(start, count, stride), :] for g in range(rows.shape[0])], axis=1
        )

    def run(c):
        for k in range(len(offsets)):
            out_copy(c, k).wait_recv()
        lanes = rows.shape[-1]
        for p in range(2):
            for s in range(src_span):
                for t in range(tgt_span):
                    for i in range(first):
                        at = p * box_count + (s * first + i) * v_count + t * second
                        piece = landed[c, s * tgt_span + t, p, 0, i].astype(jnp.float32)
                        for g in range(rows.shape[0]):
                            rows[g, pl.ds(at, second), :] = piece[:, g * lanes : (g + 1) * lanes]
        blocks = [
            [take(p * box_count + i * v_count, v_count, 1) for i in range(u_count)]
            for p in range(2)
        ]
        u_top = u_count.bit_length() - 2
        v_top = v_count.bit_length() - 2
        for level in range(level_count):
            blocks = apply_level(modulate(blocks, phase, level), level, u_top - level)
        if c == 0:
            mirror_copy(len(offsets) - 1).wait_recv()
            for p in range(2):
                for s in range(src_span):
                    for t in range(tgt_span):
                        for i in range(first):
                            at = (s * first + i) * v_count + t * second
                            mirror[0, p, pl.ds(at, second), :] = mirror_in[
                                p, s * tgt_span + t, i
                            ].astype(jnp.float32)
            for i in range(u_count):
                at = pl.ds(i * v_count, v_count)
                both = times(
                    (mirror[0, 0, at, :], mirror[0, 1, at, :]),
                    (phase[level_count, 0, at, :], phase[level_count, 1, at, :]),
                )
                mirror[0, 0, at, :] = both[0]
                mirror[0, 1, at, :] = both[1]
        place_blocks(modulate(blocks, mirror, 0))
        blocks = [
            [take(p * box_count + i, u_count, v_count) for i in range(v_count)] for p in range(2)
        ]
        for level in range(level_count):
            n = level_count + level
            if level:
                blocks = modulate(blocks, phase, n)
            blocks = apply_level(blocks, n, v_top - level)
        place_blocks(blocks)
        for s in range(src_span):
            for t in range(tgt_span):
                for p in range(2):
                    for i in range(first):
                        at = p * box_count + t * second * u_count + s * first + i
                        back[c, s * tgt_span + t, p, 0, i] = take(at, second, u_count).astype(
                            jnp.bfloat16
                        )
        for k in range(len(offsets)):
            back_copy(c, k).start()

    for c in range(chunks):
        run(c)
    for k in range(len(offsets)):
        for c in range(chunks):
            out_copy(c, k).wait_send()
            back_copy(c, k).wait_recv()
            back_copy(c, k).wait_send()
        mirror_copy(k).wait_send()


def by_spreading(coeffs, reflection, interp, orders):
    level_count = interp.shape[1]
    order_count = interp.shape[-1]
    _, ills, first, second, coef_count = coeffs.shape
    spans = (lax.axis_size("src"), lax.axis_size("tgt"))
    places = spans[0] * spans[1]
    chunks = ills // places
    box_count = places * first * second
    lanes = min(128, coef_count)
    far = pl.BlockSpec(memory_space=pltpu.HBM)
    return pl.pallas_call(
        functools.partial(spread_kernel, spans),
        out_shape=jax.ShapeDtypeStruct(coeffs.shape, jnp.bfloat16),
        in_specs=[far] * 4,
        out_specs=pl.BlockSpec(memory_space=pltpu.VMEM),
        scratch_shapes=[
            pltpu.VMEM(reflection.shape, jnp.float32),
            pltpu.VMEM(interp.shape, jnp.float32),
            pltpu.VMEM((1, coef_count), jnp.int32),
            pltpu.VMEM((chunks, places, 2, 1, first, second, coef_count), jnp.bfloat16),
            pltpu.VMEM((chunks, places, 2, 1, first, second, coef_count), jnp.bfloat16),
            pltpu.VMEM(reflection.shape, jnp.bfloat16),
            pltpu.VMEM((2, places, first, second, coef_count), jnp.bfloat16),
            pltpu.VMEM((coef_count // lanes, 2 * box_count, lanes), jnp.float32),
            pltpu.VMEM((3, 8 * level_count * order_count, coef_count), jnp.float32),
            pltpu.VMEM((2 * level_count, 2, box_count, coef_count), jnp.float32),
            pltpu.VMEM((1, 2, box_count, coef_count), jnp.float32),
            pltpu.VMEM((2 * level_count, 2 * coef_count, 2 * coef_count), jnp.bfloat16),
            pltpu.SemaphoreType.DMA((3,)),
            pltpu.SemaphoreType.DMA((chunks, places)),
            pltpu.SemaphoreType.DMA((chunks, places)),
            pltpu.SemaphoreType.DMA((chunks, places)),
            pltpu.SemaphoreType.DMA((chunks, places)),
            pltpu.SemaphoreType.DMA((places,)),
            pltpu.SemaphoreType.DMA((places,)),
        ],
        compiler_params=pltpu.CompilerParams(
            collective_id=0, has_side_effects=True, vmem_limit_bytes=40 * 2**20
        ),
        name="butterfly",
    )(coeffs, reflection, interp, orders.reshape(1, coef_count))


def on_device(coeffs, reflection, interp, orders):
    level_count = interp.shape[1]
    _, ills, first, second, _ = coeffs.shape
    spans = (lax.axis_size("src"), lax.axis_size("tgt"))
    covers = spans[0] * first == 2**level_count and spans[1] * second == 2**level_count
    if covers and ills % (spans[0] * spans[1]) == 0 and lax.axis_size("ill") == 2:
        return by_spreading(coeffs, reflection, interp, orders)
    return by_swaps(coeffs, reflection, interp, orders)


def solution(mesh):
    in_specs = (
        P(None, ("groups", "ill"), "src", "tgt", None),
        P(None, ("groups", "src"), "tgt", None),
        P(),
        P(),
    )
    out_specs = P(None, ("groups", "ill"), "src", "tgt", None)
    return jax.shard_map(
        on_device, mesh=mesh, in_specs=in_specs, out_specs=out_specs, check_vma=False
    )
```

```python
import functools
import math

import jax
import jax.numpy as jnp
from jax import lax
from jax.experimental import pallas as pl
from jax.experimental.pallas import tpu as pltpu
from jax.sharding import PartitionSpec as P

PHASE_RATE = 0.3
ALONG_SECOND = 1.7
DIRECTIONS = ((0.6, 0.48, 0.64), (-0.36, 0.8, 0.48))
SHARES = (2, 4, 5, 5)
LEAD = 3
LAG = 2
MESH = pl.DeviceIdType.MESH


def level_plan(level_count, boxes, sizes):
    plan = []
    for operator, axis in enumerate(("src", "tgt")):
        local_bits = boxes[operator].bit_length() - 1
        top_bit = (boxes[operator] * sizes[operator]).bit_length() - 2
        row_span = boxes[1] if operator == 0 else 1
        for level in range(level_count):
            bit = top_bit - level
            if bit >= local_bits:
                plan.append((operator, level, axis, 2 ** (bit - local_bits)))
            else:
                plan.append((operator, level, None, row_span * 2**bit))
    return plan


def own_bit(axis, mask):
    return lax.rem(lax.div(lax.axis_index(axis), mask), 2)


def partner_of(axis, mask):
    return lax.axis_index(axis) + mask * (1 - 2 * own_bit(axis, mask))


def swap_kernel(
    plan,
    boxes,
    sizes,
    coeffs,
    reflection_far,
    interp_far,
    orders_far,
    out,
    own,
    reflection,
    interp,
    orders,
    landed,
    held,
    sent,
    total,
    rows,
    spread,
    phase,
    weight,
    mirror,
    own_sem,
    send_sem,
    recv_sem,
):
    order_count = interp.shape[-1]
    coef_count = coeffs.shape[-1]
    first, second = boxes
    tile = first * second
    chunks = len(sizes)
    starts = [sum(sizes[:c]) for c in range(chunks)]
    swaps = [n for n, item in enumerate(plan) if item[2] is not None]

    def chunk(c):
        return pl.ds(2 * tile * starts[c], 2 * tile * sizes[c])

    barrier = pltpu.get_barrier_semaphore()
    for n in swaps:
        axis, mask = plan[n][2:]
        pl.semaphore_signal(
            barrier, inc=1, device_id={axis: partner_of(axis, mask)}, device_id_type=MESH
        )
    pl.semaphore_wait(barrier, len(swaps))

    def raw_copy(c):
        axis, mask = plan[0][2:]
        return pltpu.make_async_remote_copy(
            src_ref=coeffs.at[:, pl.ds(starts[c], sizes[c])],
            dst_ref=landed.at[:, pl.ds(starts[c], sizes[c])],
            send_sem=send_sem.at[0, c],
            recv_sem=recv_sem.at[0, c],
            device_id={axis: partner_of(axis, mask)},
            device_id_type=MESH,
        )

    def state_copy(s, c):
        axis, mask = plan[swaps[s]][2:]
        return pltpu.make_async_remote_copy(
            src_ref=sent.at[s - 1, chunk(c)],
            dst_ref=held.at[s - 1, chunk(c)],
            send_sem=send_sem.at[s, c],
            recv_sem=recv_sem.at[s, c],
            device_id={axis: partner_of(axis, mask)},
            device_id_type=MESH,
        )

    lead = min(LEAD, chunks) if len(swaps) > 1 else chunks
    for c in range(lead):
        raw_copy(c).start()
    own_copy = pltpu.make_async_copy(coeffs, own, own_sem.at[0])
    near = [
        pltpu.make_async_copy(orders_far, orders, own_sem.at[1]),
        pltpu.make_async_copy(interp_far, interp, own_sem.at[2]),
        pltpu.make_async_copy(reflection_far, reflection, own_sem.at[3]),
    ]
    for copy in near:
        copy.start()
    own_copy.start()
    near[0].wait()

    digits = (
        lax.div(orders[...], order_count * order_count),
        lax.rem(lax.div(orders[...], order_count), order_count),
        lax.rem(orders[...], order_count),
    )
    values = [
        jnp.cos(math.pi * (2.0 * d.astype(jnp.float32) + 1.0) / (2.0 * order_count))
        for d in digits
    ]
    products = []
    for direction in DIRECTIONS:
        summed = direction[0] * values[0] + direction[1] * values[1]
        products.append(summed + direction[2] * values[2])
    row = lax.broadcasted_iota(jnp.int32, (tile, coef_count), 0)

    def fill_phase(slot, operator, level, u_start, v_start):
        u = (lax.div(row, second) + u_start).astype(jnp.float32)
        v = (lax.rem(row, second) + v_start).astype(jnp.float32)
        position = (u + 0.5) + ALONG_SECOND * (v + 0.5)
        angle = (PHASE_RATE * (level + 1)) * position * products[operator]
        phase[slot, 0] = jnp.cos(angle).astype(jnp.bfloat16).astype(jnp.float32)
        phase[slot, 1] = jnp.sin(angle).astype(jnp.bfloat16).astype(jnp.float32)

    u_own = lax.axis_index("src") * first
    v_own = lax.axis_index("tgt") * second
    fill_phase(0, plan[0][0], plan[0][1], u_own, v_own)

    column = lax.broadcasted_iota(jnp.int32, (order_count, coef_count), 1)
    point = lax.broadcasted_iota(jnp.int32, (order_count, coef_count), 0)
    column_digits = (
        lax.div(column, order_count * order_count),
        lax.rem(lax.div(column, order_count), order_count),
        lax.rem(column, order_count),
    )
    near[1].wait()
    for d in range(3):
        selector = (point == column_digits[d]).astype(jnp.float32)
        factors = interp[:, :, :, :, d].reshape(-1, order_count, order_count)
        factors = jnp.swapaxes(factors, 1, 2).reshape(-1, order_count)
        spread[d] = jnp.dot(
            factors, selector, precision=lax.Precision.HIGHEST,
            preferred_element_type=jnp.float32,
        )

    square = order_count * order_count

    def build(slot, index):
        where = pl.ds(pl.multiple_of(index * order_count, order_count), order_count)
        first_factor = spread[0, where, :]
        second_factor = spread[1, where, :]
        third_factor = spread[2, where, :]
        for a in range(order_count):
            pair = first_factor[a : a + 1, :] * second_factor
            block = pair[:, None, :] * third_factor[None, :, :]
            weight[slot, pl.ds(a * square, square), :] = block.reshape(
                square, coef_count
            ).astype(jnp.bfloat16)

    level_count = interp.shape[1]
    slots = []
    used = 0
    for item in plan:
        slots.append(used)
        used += 2 if item[2] is not None else 4

    def build_level(n):
        operator, level, axis, mask = plan[n]
        base = (operator * level_count + level) * 4
        if axis is None:
            def step(j, carry):
                build(slots[n] + j, base + j)
                return carry
            lax.fori_loop(0, 4, step, 0)
        else:
            bit = own_bit(axis, mask)

            def step(j, carry):
                child = bit + j - 2 * bit * j
                build(slots[n] + j, base + 2 * bit + child)
                return carry
            lax.fori_loop(0, 2, step, 0)

    def dot(left, slot):
        return jnp.dot(left, weight[slot], preferred_element_type=jnp.float32)

    def modulate(value, cos_part, sin_part):
        half = value.shape[0] // 2
        shape = (half // tile, tile, coef_count)
        real = value[:half].reshape(shape)
        imag = value[half:].reshape(shape)
        new_real = cos_part * real - sin_part * imag
        new_imag = cos_part * imag + sin_part * real
        return jnp.concatenate(
            [new_real.reshape(half, coef_count), new_imag.reshape(half, coef_count)], axis=0
        ).astype(jnp.bfloat16)

    def gather_rows(ref, c):
        for p in range(2):
            for i in range(sizes[c]):
                for u in range(first):
                    at = (p * sizes[c] + i) * tile + u * second
                    rows[pl.ds(at, second), :] = ref[p, starts[c] + i, u].astype(jnp.float32)
        return rows[: 2 * sizes[c] * tile, :]

    build_level(0)
    own_copy.wait()

    for c in range(chunks):
        moved = modulate(gather_rows(own, c), phase[0, 0], phase[0, 1])
        total[0, chunk(c), :] = dot(moved, slots[0])

    axis, mask = plan[0][2:]
    shift = (partner_of(axis, mask) - lax.axis_index(axis)) * (
        first if axis == "src" else second
    )
    fill_phase(
        len(plan),
        plan[0][0],
        plan[0][1],
        u_own + (shift if axis == "src" else 0),
        v_own + (shift if axis == "tgt" else 0),
    )
    ends = [0] + swaps[1:] + [len(plan) - 1]

    def prepare(s):
        for n in range(ends[s] + 1, ends[s + 1] + 1):
            fill_phase(n, plan[n][0], plan[n][1], u_own, v_own)
            build_level(n)

    prepare(0)
    near[2].wait()
    for p in range(2):
        for u in range(first):
            mirror[p, pl.ds(u * second, second), :] = reflection[p, u]

    def stage(s, c):
        n = swaps[s]
        if s == 0:
            raw_copy(c).wait_recv()
            value = gather_rows(landed, c)
            received = modulate(value, phase[len(plan), 0], phase[len(plan), 1])
        else:
            state_copy(s, c).wait_recv()
            received = held[s - 1, chunk(c), :]
        chunk_rows = 2 * tile * sizes[c]
        row_index = lax.broadcasted_iota(jnp.int32, (chunk_rows, coef_count), 0)
        summed = total[s, chunk(c), :] + dot(received, slots[n] + 1)
        state = summed.astype(jnp.bfloat16).astype(jnp.float32)
        last = swaps[s + 1] if s + 1 < len(swaps) else len(plan)
        for m in range(n + 1, last + 1):
            before = plan[m - 1][0]
            if before == 0 and (m == len(plan) or plan[m][0] == 1):
                state = (
                    modulate(state, mirror[0], mirror[1]).astype(jnp.float32)
                )
            if m == len(plan):
                break
            moved = modulate(state, phase[m, 0], phase[m, 1])
            if m == last:
                sent[s, chunk(c), :] = moved
                state_copy(s + 1, c).start()
                if s == 0 and c + lead < chunks:
                    raw_copy(c + lead).start()
                total[s + 1, chunk(c), :] = dot(moved, slots[m])
                return
            span = plan[m][3]
            upper_row = lax.rem(lax.div(row_index, span), 2) == 1
            wide = moved.astype(jnp.float32)
            lower = jnp.where(upper_row, pltpu.roll(wide, span, 0), wide).astype(jnp.bfloat16)
            upper = jnp.where(
                upper_row, wide, pltpu.roll(wide, chunk_rows - span, 0)
            ).astype(jnp.bfloat16)
            low = dot(lower, slots[m]) + dot(upper, slots[m] + 1)
            high = dot(lower, slots[m] + 2) + dot(upper, slots[m] + 3)
            state = jnp.where(upper_row, high, low).astype(jnp.bfloat16).astype(jnp.float32)
        result = state.astype(jnp.bfloat16).reshape(2, sizes[c], tile, coef_count)
        out[:, pl.ds(starts[c], sizes[c])] = result

    for t in range(chunks + LAG * (len(swaps) - 1)):
        for s in range(len(swaps)):
            if 0 <= t - LAG * s < chunks:
                stage(s, t - LAG * s)
        if 1 <= t + 1 < len(swaps):
            prepare(t + 1)

    for c in range(chunks):
        raw_copy(c).wait_send()
        for s in range(1, len(swaps)):
            state_copy(s, c).wait_send()


def by_swaps(coeffs, reflection, interp, orders):
    level_count = interp.shape[1]
    order_count = interp.shape[-1]
    _, ills, first, second, coef_count = coeffs.shape
    sizes_of = [ills * share // sum(SHARES) for share in SHARES]
    sizes_of[0] += ills - sum(sizes_of)
    sizes_of = [size for size in sizes_of if size > 0]
    chunks = len(sizes_of)
    tile = first * second
    sizes = (lax.axis_size("src"), lax.axis_size("tgt"))
    plan = level_plan(level_count, (first, second), sizes)
    swap_count = sum(item[2] is not None for item in plan)
    slot_count = 2 * swap_count + 4 * (len(plan) - swap_count)
    state_rows = 2 * ills * tile
    later = max(swap_count - 1, 1)
    whole = pl.BlockSpec(memory_space=pltpu.VMEM)
    result = pl.pallas_call(
        functools.partial(swap_kernel, plan, (first, second), sizes_of),
        out_shape=jax.ShapeDtypeStruct((2, ills, tile, coef_count), jnp.bfloat16),
        in_specs=[pl.BlockSpec(memory_space=pl.ANY)] * 4,
        out_specs=whole,
        scratch_shapes=[
            pltpu.VMEM(coeffs.shape, jnp.bfloat16),
            pltpu.VMEM(reflection.shape, jnp.float32),
            pltpu.VMEM(interp.shape, jnp.float32),
            pltpu.VMEM((1, coef_count), jnp.int32),
            pltpu.VMEM(coeffs.shape, jnp.bfloat16),
            pltpu.VMEM((later, state_rows, coef_count), jnp.bfloat16),
            pltpu.VMEM((later, state_rows, coef_count), jnp.bfloat16),
            pltpu.VMEM((swap_count, state_rows, coef_count), jnp.float32),
            pltpu.VMEM((2 * tile * max(sizes_of), coef_count), jnp.float32),
            pltpu.VMEM((3, 8 * level_count * order_count, coef_count), jnp.float32),
            pltpu.VMEM((len(plan) + 1, 2, tile, coef_count), jnp.float32),
            pltpu.VMEM((slot_count, coef_count, coef_count), jnp.bfloat16),
            pltpu.VMEM((2, tile, coef_count), jnp.float32),
            pltpu.SemaphoreType.DMA((4,)),
            pltpu.SemaphoreType.DMA((swap_count, chunks)),
            pltpu.SemaphoreType.DMA((swap_count, chunks)),
        ],
        compiler_params=pltpu.CompilerParams(
            collective_id=0, has_side_effects=True, vmem_limit_bytes=60 * 2**20
        ),
        name="butterfly",
    )(coeffs, reflection, interp, orders.reshape(1, coef_count))
    return result.reshape(coeffs.shape)


def flipped(axis, mask):
    index = lax.axis_index(axis)
    for bit in range(mask.bit_length()):
        if mask >> bit & 1:
            index = index + 2**bit * (1 - 2 * lax.rem(lax.div(index, 2**bit), 2))
    return index


def spread_kernel(
    spans,
    coeffs,
    reflection_far,
    interp_far,
    orders_far,
    out,
    reflection,
    interp,
    orders,
    landed,
    back,
    mirror_out,
    mirror_in,
    rows,
    spread,
    phase,
    mirror,
    weight,
    near_sem,
    send_sem,
    recv_sem,
    back_send_sem,
    back_recv_sem,
    mirror_send_sem,
    mirror_recv_sem,
):
    src_span, tgt_span = spans
    chunks = landed.shape[0]
    order_count = interp.shape[-1]
    level_count = interp.shape[1]
    coef_count = coeffs.shape[-1]
    first, second = coeffs.shape[2:4]
    u_count, v_count = src_span * first, tgt_span * second
    box_count = u_count * v_count
    square = order_count * order_count

    u_home = lax.axis_index("src")
    v_home = lax.axis_index("tgt")
    core = lax.axis_index("ill")
    home = u_home * tgt_span + v_home
    offsets = [(du, dv) for du in reversed(range(src_span)) for dv in reversed(range(tgt_span))]

    def device(k):
        return {
            "src": flipped("src", offsets[k][0]),
            "tgt": flipped("tgt", offsets[k][1]),
            "ill": 1 - core,
        }

    def place(k):
        return flipped("src", offsets[k][0]) * tgt_span + flipped("tgt", offsets[k][1])

    barrier = pltpu.get_barrier_semaphore()
    for k in range(len(offsets)):
        pl.semaphore_signal(barrier, inc=1, device_id=device(k), device_id_type=MESH)

    near = [
        pltpu.make_async_copy(orders_far, orders, near_sem.at[0]),
        pltpu.make_async_copy(reflection_far, reflection, near_sem.at[1]),
        pltpu.make_async_copy(interp_far, interp, near_sem.at[2]),
    ]
    for copy in near:
        copy.start()

    def out_copy(c, k):
        return pltpu.make_async_remote_copy(
            src_ref=coeffs.at[:, pl.ds(place(k) * chunks + c, 1)],
            dst_ref=landed.at[c, home],
            send_sem=send_sem.at[c, k],
            recv_sem=recv_sem.at[c, k],
            device_id=device(k),
            device_id_type=MESH,
        )

    def back_copy(c, k):
        return pltpu.make_async_remote_copy(
            src_ref=back.at[c, place(k)],
            dst_ref=out.at[:, pl.ds(home * chunks + c, 1)],
            send_sem=back_send_sem.at[c, k],
            recv_sem=back_recv_sem.at[c, k],
            device_id=device(k),
            device_id_type=MESH,
        )

    def mirror_copy(k):
        if offsets[k] == (0, 0):
            source, target = mirror_in.at[1 - core], mirror_in.at[1 - core]
        else:
            source, target = mirror_out.at[core], mirror_in.at[core, home]
        return pltpu.make_async_remote_copy(
            src_ref=source,
            dst_ref=target,
            send_sem=mirror_send_sem.at[k],
            recv_sem=mirror_recv_sem.at[k],
            device_id=device(k),
            device_id_type=MESH,
        )

    near[1].wait()
    mirror_out[...] = reflection[...].astype(jnp.bfloat16)
    mirror_in[1 - core, home] = mirror_out[1 - core]

    pl.semaphore_wait(barrier, len(offsets))
    for k in range(len(offsets)):
        out_copy(0, k).start()
    for k in range(len(offsets) - 1):
        mirror_copy(k).start()
    for c in range(1, chunks):
        for k in range(len(offsets)):
            out_copy(c, k).start()

    near[0].wait()
    digits = (
        lax.div(orders[...], square),
        lax.rem(lax.div(orders[...], order_count), order_count),
        lax.rem(orders[...], order_count),
    )
    values = [
        jnp.cos(math.pi * (2.0 * d.astype(jnp.float32) + 1.0) / (2.0 * order_count))
        for d in digits
    ]

    def times(left, right):
        return (
            left[0] * right[0] - left[1] * right[1],
            left[0] * right[1] + left[1] * right[0],
        )

    def fill_phases(operator):
        direction = DIRECTIONS[operator]
        node = direction[0] * values[0] + direction[1] * values[1]
        node = node + direction[2] * values[2]
        turns = []
        for count, rate in ((u_count, PHASE_RATE), (v_count, PHASE_RATE * ALONG_SECOND)):
            position = lax.broadcasted_iota(jnp.int32, (count, coef_count), 0)
            angle = rate * (position.astype(jnp.float32) + 0.5) * node
            turns.append((jnp.cos(angle), jnp.sin(angle)))
        u_turn, v_turn = turns
        u_now, v_now = u_turn, v_turn
        for level in range(level_count):
            if level:
                u_now, v_now = times(u_now, u_turn), times(v_now, v_turn)
            n = operator * level_count + level
            outer, inner = (u_now, v_now) if n <= level_count else (v_now, u_now)
            span = inner[0].shape[0]
            for i in range(outer[0].shape[0]):
                turn = times((outer[0][i : i + 1], outer[1][i : i + 1]), inner)
                phase[n, 0, pl.ds(i * span, span), :] = turn[0]
                phase[n, 1, pl.ds(i * span, span), :] = turn[1]

    for operator in range(2):
        fill_phases(operator)

    column = lax.broadcasted_iota(jnp.int32, (order_count, coef_count), 1)
    point = lax.broadcasted_iota(jnp.int32, (order_count, coef_count), 0)
    column_digits = (
        lax.div(column, square),
        lax.rem(lax.div(column, order_count), order_count),
        lax.rem(column, order_count),
    )
    near[2].wait()
    for d in range(3):
        selector = (point == column_digits[d]).astype(jnp.float32)
        factors = interp[:, :, :, :, d].reshape(-1, order_count, order_count)
        factors = jnp.swapaxes(factors, 1, 2).reshape(-1, order_count)
        spread[d] = jnp.dot(
            factors, selector, precision=lax.Precision.HIGHEST,
            preferred_element_type=jnp.float32,
        )

    def build(index, carry):
        where = pl.ds(pl.multiple_of(index * order_count, order_count), order_count)
        n = lax.div(index, 4)
        side = lax.rem(lax.div(index, 2), 2)
        child = lax.rem(index, 2)
        columns = pl.ds(pl.multiple_of(side * coef_count, coef_count), coef_count)
        first_factor = spread[0, where, :]
        second_factor = spread[1, where, :]
        third_factor = spread[2, where, :]
        for a in range(order_count):
            pair = first_factor[a : a + 1, :] * second_factor
            block = pair[:, None, :] * third_factor[None, :, :]
            at = pl.multiple_of(child * coef_count + a * square, square)
            weight[n, pl.ds(at, square), columns] = block.reshape(square, coef_count).astype(
                jnp.bfloat16
            )
        return carry

    lax.fori_loop(0, 4 * 2 * level_count, build, 0)

    for k in range(len(offsets) - 1):
        mirror_copy(k).wait_recv()
    mirror_copy(len(offsets) - 1).start()

    def modulate(blocks, table, n):
        result = [[], []]
        for i, (real, imag) in enumerate(zip(*blocks)):
            span = real.shape[0]
            at = pl.ds(i * span, span)
            new = times((table[n, 0, at, :], table[n, 1, at, :]), (real, imag))
            result[0].append(new[0])
            result[1].append(new[1])
        return result

    def apply_level(blocks, n, bit):
        count = len(blocks[0])
        low = [i for i in range(count) if not i >> bit & 1]
        parts = [
            jnp.concatenate([blocks[p][i + side * 2**bit] for p in range(2) for i in low], axis=0)
            for side in range(2)
        ]
        left = jnp.concatenate(parts, axis=1).astype(jnp.bfloat16)
        result = jnp.dot(left, weight[n], preferred_element_type=jnp.float32)
        new = [[None] * count, [None] * count]
        span = blocks[0][0].shape[0]
        for p in range(2):
            for at, i in enumerate(low):
                start = (p * len(low) + at) * span
                for side in range(2):
                    new[p][i + side * 2**bit] = result[
                        start : start + span, side * coef_count : (side + 1) * coef_count
                    ]
        return new

    def place_blocks(blocks):
        for p in range(2):
            for i, block in enumerate(blocks[p]):
                span = block.shape[0]
                lanes = rows.shape[-1]
                for g in range(rows.shape[0]):
                    rows[g, pl.ds(p * box_count + i * span, span), :] = block[
                        :, g * lanes : (g + 1) * lanes
                    ]

    def take(start, count, stride):
        return jnp.concatenate(
            [rows[g, pl.ds(start, count, stride), :] for g in range(rows.shape[0])], axis=1
        )

    def run(c):
        for k in range(len(offsets)):
            out_copy(c, k).wait_recv()
        lanes = rows.shape[-1]
        for p in range(2):
            for s in range(src_span):
                for t in range(tgt_span):
                    for i in range(first):
                        at = p * box_count + (s * first + i) * v_count + t * second
                        piece = landed[c, s * tgt_span + t, p, 0, i].astype(jnp.float32)
                        for g in range(rows.shape[0]):
                            rows[g, pl.ds(at, second), :] = piece[:, g * lanes : (g + 1) * lanes]
        blocks = [
            [take(p * box_count + i * v_count, v_count, 1) for i in range(u_count)]
            for p in range(2)
        ]
        u_top = u_count.bit_length() - 2
        v_top = v_count.bit_length() - 2
        for level in range(level_count):
            blocks = apply_level(modulate(blocks, phase, level), level, u_top - level)
        if c == 0:
            mirror_copy(len(offsets) - 1).wait_recv()
            for p in range(2):
                for s in range(src_span):
                    for t in range(tgt_span):
                        for i in range(first):
                            at = (s * first + i) * v_count + t * second
                            mirror[0, p, pl.ds(at, second), :] = mirror_in[
                                p, s * tgt_span + t, i
                            ].astype(jnp.float32)
            for i in range(u_count):
                at = pl.ds(i * v_count, v_count)
                both = times(
                    (mirror[0, 0, at, :], mirror[0, 1, at, :]),
                    (phase[level_count, 0, at, :], phase[level_count, 1, at, :]),
                )
                mirror[0, 0, at, :] = both[0]
                mirror[0, 1, at, :] = both[1]
        place_blocks(modulate(blocks, mirror, 0))
        blocks = [
            [take(p * box_count + i, u_count, v_count) for i in range(v_count)] for p in range(2)
        ]
        for level in range(level_count):
            n = level_count + level
            if level:
                blocks = modulate(blocks, phase, n)
            blocks = apply_level(blocks, n, v_top - level)
        place_blocks(blocks)
        for s in range(src_span):
            for t in range(tgt_span):
                for p in range(2):
                    for i in range(first):
                        at = p * box_count + t * second * u_count + s * first + i
                        back[c, s * tgt_span + t, p, 0, i] = take(at, second, u_count).astype(
                            jnp.bfloat16
                        )
        for k in range(len(offsets)):
            back_copy(c, k).start()

    for c in range(chunks):
        run(c)
    for k in range(len(offsets)):
        for c in range(chunks):
            out_copy(c, k).wait_send()
            back_copy(c, k).wait_recv()
            back_copy(c, k).wait_send()
        mirror_copy(k).wait_send()


def by_spreading(coeffs, reflection, interp, orders):
    level_count = interp.shape[1]
    order_count = interp.shape[-1]
    _, ills, first, second, coef_count = coeffs.shape
    spans = (lax.axis_size("src"), lax.axis_size("tgt"))
    places = spans[0] * spans[1]
    chunks = ills // places
    box_count = places * first * second
    lanes = min(128, coef_count)
    far = pl.BlockSpec(memory_space=pltpu.HBM)
    operands = [
        pltpu.with_memory_space_constraint(operand, pltpu.HBM)
        for operand in (coeffs, reflection, interp, orders.reshape(1, coef_count))
    ]
    return pl.pallas_call(
        functools.partial(spread_kernel, spans),
        out_shape=jax.ShapeDtypeStruct(coeffs.shape, jnp.bfloat16),
        in_specs=[far] * 4,
        out_specs=pl.BlockSpec(memory_space=pltpu.VMEM),
        scratch_shapes=[
            pltpu.VMEM(reflection.shape, jnp.float32),
            pltpu.VMEM(interp.shape, jnp.float32),
            pltpu.VMEM((1, coef_count), jnp.int32),
            pltpu.VMEM((chunks, places, 2, 1, first, second, coef_count), jnp.bfloat16),
            pltpu.VMEM((chunks, places, 2, 1, first, second, coef_count), jnp.bfloat16),
            pltpu.VMEM(reflection.shape, jnp.bfloat16),
            pltpu.VMEM((2, places, first, second, coef_count), jnp.bfloat16),
            pltpu.VMEM((coef_count // lanes, 2 * box_count, lanes), jnp.float32),
            pltpu.VMEM((3, 8 * level_count * order_count, coef_count), jnp.float32),
            pltpu.VMEM((2 * level_count, 2, box_count, coef_count), jnp.float32),
            pltpu.VMEM((1, 2, box_count, coef_count), jnp.float32),
            pltpu.VMEM((2 * level_count, 2 * coef_count, 2 * coef_count), jnp.bfloat16),
            pltpu.SemaphoreType.DMA((3,)),
            pltpu.SemaphoreType.DMA((chunks, places)),
            pltpu.SemaphoreType.DMA((chunks, places)),
            pltpu.SemaphoreType.DMA((chunks, places)),
            pltpu.SemaphoreType.DMA((chunks, places)),
            pltpu.SemaphoreType.DMA((places,)),
            pltpu.SemaphoreType.DMA((places,)),
        ],
        compiler_params=pltpu.CompilerParams(
            collective_id=0, has_side_effects=True, vmem_limit_bytes=40 * 2**20
        ),
        name="butterfly",
    )(*operands)


def on_device(coeffs, reflection, interp, orders):
    level_count = interp.shape[1]
    _, ills, first, second, _ = coeffs.shape
    spans = (lax.axis_size("src"), lax.axis_size("tgt"))
    covers = spans[0] * first == 2**level_count and spans[1] * second == 2**level_count
    if covers and ills % (spans[0] * spans[1]) == 0 and lax.axis_size("ill") == 2:
        return by_spreading(coeffs, reflection, interp, orders)
    return by_swaps(coeffs, reflection, interp, orders)


def solution(mesh):
    in_specs = (
        P(None, ("groups", "ill"), "src", "tgt", None),
        P(None, ("groups", "src"), "tgt", None),
        P(),
        P(),
    )
    out_specs = P(None, ("groups", "ill"), "src", "tgt", None)
    return jax.shard_map(
        on_device, mesh=mesh, in_specs=in_specs, out_specs=out_specs, check_vma=False
    )
```

```python
import functools
import math

import jax
import jax.numpy as jnp
from jax import lax
from jax.experimental import pallas as pl
from jax.experimental.pallas import tpu as pltpu
from jax.sharding import PartitionSpec as P

PHASE_RATE = 0.3
ALONG_SECOND = 1.7
DIRECTIONS = ((0.6, 0.48, 0.64), (-0.36, 0.8, 0.48))
SHARES = (2, 4, 5, 5)
LEAD = 3
LAG = 2
MESH = pl.DeviceIdType.MESH


def level_plan(level_count, boxes, sizes):
    plan = []
    for operator, axis in enumerate(("src", "tgt")):
        local_bits = boxes[operator].bit_length() - 1
        top_bit = (boxes[operator] * sizes[operator]).bit_length() - 2
        row_span = boxes[1] if operator == 0 else 1
        for level in range(level_count):
            bit = top_bit - level
            if bit >= local_bits:
                plan.append((operator, level, axis, 2 ** (bit - local_bits)))
            else:
                plan.append((operator, level, None, row_span * 2**bit))
    return plan


def own_bit(axis, mask):
    return lax.rem(lax.div(lax.axis_index(axis), mask), 2)


def partner_of(axis, mask):
    return lax.axis_index(axis) + mask * (1 - 2 * own_bit(axis, mask))


def swap_kernel(
    plan,
    boxes,
    sizes,
    coeffs,
    reflection_far,
    interp_far,
    orders_far,
    out,
    own,
    reflection,
    interp,
    orders,
    landed,
    held,
    sent,
    total,
    rows,
    spread,
    phase,
    weight,
    mirror,
    own_sem,
    send_sem,
    recv_sem,
):
    order_count = interp.shape[-1]
    coef_count = coeffs.shape[-1]
    first, second = boxes
    tile = first * second
    chunks = len(sizes)
    starts = [sum(sizes[:c]) for c in range(chunks)]
    swaps = [n for n, item in enumerate(plan) if item[2] is not None]

    def chunk(c):
        return pl.ds(2 * tile * starts[c], 2 * tile * sizes[c])

    barrier = pltpu.get_barrier_semaphore()
    for n in swaps:
        axis, mask = plan[n][2:]
        pl.semaphore_signal(
            barrier, inc=1, device_id={axis: partner_of(axis, mask)}, device_id_type=MESH
        )
    pl.semaphore_wait(barrier, len(swaps))

    def raw_copy(c):
        axis, mask = plan[0][2:]
        return pltpu.make_async_remote_copy(
            src_ref=coeffs.at[:, pl.ds(starts[c], sizes[c])],
            dst_ref=landed.at[:, pl.ds(starts[c], sizes[c])],
            send_sem=send_sem.at[0, c],
            recv_sem=recv_sem.at[0, c],
            device_id={axis: partner_of(axis, mask)},
            device_id_type=MESH,
        )

    def state_copy(s, c):
        axis, mask = plan[swaps[s]][2:]
        return pltpu.make_async_remote_copy(
            src_ref=sent.at[s - 1, chunk(c)],
            dst_ref=held.at[s - 1, chunk(c)],
            send_sem=send_sem.at[s, c],
            recv_sem=recv_sem.at[s, c],
            device_id={axis: partner_of(axis, mask)},
            device_id_type=MESH,
        )

    lead = min(LEAD, chunks) if len(swaps) > 1 else chunks
    for c in range(lead):
        raw_copy(c).start()
    own_copy = pltpu.make_async_copy(coeffs, own, own_sem.at[0])
    near = [
        pltpu.make_async_copy(orders_far, orders, own_sem.at[1]),
        pltpu.make_async_copy(interp_far, interp, own_sem.at[2]),
        pltpu.make_async_copy(reflection_far, reflection, own_sem.at[3]),
    ]
    for copy in near:
        copy.start()
    own_copy.start()
    near[0].wait()

    digits = (
        lax.div(orders[...], order_count * order_count),
        lax.rem(lax.div(orders[...], order_count), order_count),
        lax.rem(orders[...], order_count),
    )
    values = [
        jnp.cos(math.pi * (2.0 * d.astype(jnp.float32) + 1.0) / (2.0 * order_count))
        for d in digits
    ]
    products = []
    for direction in DIRECTIONS:
        summed = direction[0] * values[0] + direction[1] * values[1]
        products.append(summed + direction[2] * values[2])
    row = lax.broadcasted_iota(jnp.int32, (tile, coef_count), 0)

    def fill_phase(slot, operator, level, u_start, v_start):
        u = (lax.div(row, second) + u_start).astype(jnp.float32)
        v = (lax.rem(row, second) + v_start).astype(jnp.float32)
        position = (u + 0.5) + ALONG_SECOND * (v + 0.5)
        angle = (PHASE_RATE * (level + 1)) * position * products[operator]
        phase[slot, 0] = jnp.cos(angle).astype(jnp.bfloat16).astype(jnp.float32)
        phase[slot, 1] = jnp.sin(angle).astype(jnp.bfloat16).astype(jnp.float32)

    u_own = lax.axis_index("src") * first
    v_own = lax.axis_index("tgt") * second
    fill_phase(0, plan[0][0], plan[0][1], u_own, v_own)

    column = lax.broadcasted_iota(jnp.int32, (order_count, coef_count), 1)
    point = lax.broadcasted_iota(jnp.int32, (order_count, coef_count), 0)
    column_digits = (
        lax.div(column, order_count * order_count),
        lax.rem(lax.div(column, order_count), order_count),
        lax.rem(column, order_count),
    )
    near[1].wait()
    for d in range(3):
        selector = (point == column_digits[d]).astype(jnp.float32)
        factors = interp[:, :, :, :, d].reshape(-1, order_count, order_count)
        factors = jnp.swapaxes(factors, 1, 2).reshape(-1, order_count)
        spread[d] = jnp.dot(
            factors, selector, precision=lax.Precision.HIGHEST,
            preferred_element_type=jnp.float32,
        )

    square = order_count * order_count

    def build(slot, index):
        where = pl.ds(pl.multiple_of(index * order_count, order_count), order_count)
        first_factor = spread[0, where, :]
        second_factor = spread[1, where, :]
        third_factor = spread[2, where, :]
        for a in range(order_count):
            pair = first_factor[a : a + 1, :] * second_factor
            block = pair[:, None, :] * third_factor[None, :, :]
            weight[slot, pl.ds(a * square, square), :] = block.reshape(
                square, coef_count
            ).astype(jnp.bfloat16)

    level_count = interp.shape[1]
    slots = []
    used = 0
    for item in plan:
        slots.append(used)
        used += 2 if item[2] is not None else 4

    def build_level(n):
        operator, level, axis, mask = plan[n]
        base = (operator * level_count + level) * 4
        if axis is None:
            def step(j, carry):
                build(slots[n] + j, base + j)
                return carry
            lax.fori_loop(0, 4, step, 0)
        else:
            bit = own_bit(axis, mask)

            def step(j, carry):
                child = bit + j - 2 * bit * j
                build(slots[n] + j, base + 2 * bit + child)
                return carry
            lax.fori_loop(0, 2, step, 0)

    def dot(left, slot):
        return jnp.dot(left, weight[slot], preferred_element_type=jnp.float32)

    def modulate(value, cos_part, sin_part):
        half = value.shape[0] // 2
        shape = (half // tile, tile, coef_count)
        real = value[:half].reshape(shape)
        imag = value[half:].reshape(shape)
        new_real = cos_part * real - sin_part * imag
        new_imag = cos_part * imag + sin_part * real
        return jnp.concatenate(
            [new_real.reshape(half, coef_count), new_imag.reshape(half, coef_count)], axis=0
        ).astype(jnp.bfloat16)

    def gather_rows(ref, c):
        for p in range(2):
            for i in range(sizes[c]):
                for u in range(first):
                    at = (p * sizes[c] + i) * tile + u * second
                    rows[pl.ds(at, second), :] = ref[p, starts[c] + i, u].astype(jnp.float32)
        return rows[: 2 * sizes[c] * tile, :]

    build_level(0)
    own_copy.wait()

    for c in range(chunks):
        moved = modulate(gather_rows(own, c), phase[0, 0], phase[0, 1])
        total[0, chunk(c), :] = dot(moved, slots[0])

    axis, mask = plan[0][2:]
    shift = (partner_of(axis, mask) - lax.axis_index(axis)) * (
        first if axis == "src" else second
    )
    fill_phase(
        len(plan),
        plan[0][0],
        plan[0][1],
        u_own + (shift if axis == "src" else 0),
        v_own + (shift if axis == "tgt" else 0),
    )
    ends = [0] + swaps[1:] + [len(plan) - 1]

    def prepare(s):
        for n in range(ends[s] + 1, ends[s + 1] + 1):
            fill_phase(n, plan[n][0], plan[n][1], u_own, v_own)
            build_level(n)

    prepare(0)
    near[2].wait()
    for p in range(2):
        for u in range(first):
            mirror[p, pl.ds(u * second, second), :] = reflection[p, u]

    def stage(s, c):
        n = swaps[s]
        if s == 0:
            raw_copy(c).wait_recv()
            value = gather_rows(landed, c)
            received = modulate(value, phase[len(plan), 0], phase[len(plan), 1])
        else:
            state_copy(s, c).wait_recv()
            received = held[s - 1, chunk(c), :]
        chunk_rows = 2 * tile * sizes[c]
        row_index = lax.broadcasted_iota(jnp.int32, (chunk_rows, coef_count), 0)
        summed = total[s, chunk(c), :] + dot(received, slots[n] + 1)
        state = summed.astype(jnp.bfloat16).astype(jnp.float32)
        last = swaps[s + 1] if s + 1 < len(swaps) else len(plan)
        for m in range(n + 1, last + 1):
            before = plan[m - 1][0]
            if before == 0 and (m == len(plan) or plan[m][0] == 1):
                state = (
                    modulate(state, mirror[0], mirror[1]).astype(jnp.float32)
                )
            if m == len(plan):
                break
            moved = modulate(state, phase[m, 0], phase[m, 1])
            if m == last:
                sent[s, chunk(c), :] = moved
                state_copy(s + 1, c).start()
                if s == 0 and c + lead < chunks:
                    raw_copy(c + lead).start()
                total[s + 1, chunk(c), :] = dot(moved, slots[m])
                return
            span = plan[m][3]
            upper_row = lax.rem(lax.div(row_index, span), 2) == 1
            wide = moved.astype(jnp.float32)
            lower = jnp.where(upper_row, pltpu.roll(wide, span, 0), wide).astype(jnp.bfloat16)
            upper = jnp.where(
                upper_row, wide, pltpu.roll(wide, chunk_rows - span, 0)
            ).astype(jnp.bfloat16)
            low = dot(lower, slots[m]) + dot(upper, slots[m] + 1)
            high = dot(lower, slots[m] + 2) + dot(upper, slots[m] + 3)
            state = jnp.where(upper_row, high, low).astype(jnp.bfloat16).astype(jnp.float32)
        result = state.astype(jnp.bfloat16).reshape(2, sizes[c], tile, coef_count)
        out[:, pl.ds(starts[c], sizes[c])] = result

    for t in range(chunks + LAG * (len(swaps) - 1)):
        for s in range(len(swaps)):
            if 0 <= t - LAG * s < chunks:
                stage(s, t - LAG * s)
        if 1 <= t + 1 < len(swaps):
            prepare(t + 1)

    for c in range(chunks):
        raw_copy(c).wait_send()
        for s in range(1, len(swaps)):
            state_copy(s, c).wait_send()


def by_swaps(coeffs, reflection, interp, orders):
    level_count = interp.shape[1]
    order_count = interp.shape[-1]
    _, ills, first, second, coef_count = coeffs.shape
    sizes_of = [ills * share // sum(SHARES) for share in SHARES]
    sizes_of[0] += ills - sum(sizes_of)
    sizes_of = [size for size in sizes_of if size > 0]
    chunks = len(sizes_of)
    tile = first * second
    sizes = (lax.axis_size("src"), lax.axis_size("tgt"))
    plan = level_plan(level_count, (first, second), sizes)
    swap_count = sum(item[2] is not None for item in plan)
    slot_count = 2 * swap_count + 4 * (len(plan) - swap_count)
    state_rows = 2 * ills * tile
    later = max(swap_count - 1, 1)
    whole = pl.BlockSpec(memory_space=pltpu.VMEM)
    result = pl.pallas_call(
        functools.partial(swap_kernel, plan, (first, second), sizes_of),
        out_shape=jax.ShapeDtypeStruct((2, ills, tile, coef_count), jnp.bfloat16),
        in_specs=[pl.BlockSpec(memory_space=pl.ANY)] * 4,
        out_specs=whole,
        scratch_shapes=[
            pltpu.VMEM(coeffs.shape, jnp.bfloat16),
            pltpu.VMEM(reflection.shape, jnp.float32),
            pltpu.VMEM(interp.shape, jnp.float32),
            pltpu.VMEM((1, coef_count), jnp.int32),
            pltpu.VMEM(coeffs.shape, jnp.bfloat16),
            pltpu.VMEM((later, state_rows, coef_count), jnp.bfloat16),
            pltpu.VMEM((later, state_rows, coef_count), jnp.bfloat16),
            pltpu.VMEM((swap_count, state_rows, coef_count), jnp.float32),
            pltpu.VMEM((2 * tile * max(sizes_of), coef_count), jnp.float32),
            pltpu.VMEM((3, 8 * level_count * order_count, coef_count), jnp.float32),
            pltpu.VMEM((len(plan) + 1, 2, tile, coef_count), jnp.float32),
            pltpu.VMEM((slot_count, coef_count, coef_count), jnp.bfloat16),
            pltpu.VMEM((2, tile, coef_count), jnp.float32),
            pltpu.SemaphoreType.DMA((4,)),
            pltpu.SemaphoreType.DMA((swap_count, chunks)),
            pltpu.SemaphoreType.DMA((swap_count, chunks)),
        ],
        compiler_params=pltpu.CompilerParams(
            collective_id=0, has_side_effects=True, vmem_limit_bytes=60 * 2**20
        ),
        name="butterfly",
    )(coeffs, reflection, interp, orders.reshape(1, coef_count))
    return result.reshape(coeffs.shape)


def flipped(axis, mask):
    index = lax.axis_index(axis)
    for bit in range(mask.bit_length()):
        if mask >> bit & 1:
            index = index + 2**bit * (1 - 2 * lax.rem(lax.div(index, 2**bit), 2))
    return index


def spread_kernel(
    spans,
    coeffs,
    reflection_far,
    interp_far,
    orders_far,
    out,
    reflection,
    interp,
    orders,
    landed,
    back,
    mirror_out,
    mirror_in,
    rows,
    spread,
    phase,
    mirror,
    weight,
    near_sem,
    send_sem,
    recv_sem,
    back_send_sem,
    back_recv_sem,
    mirror_send_sem,
    mirror_recv_sem,
):
    src_span, tgt_span = spans
    chunks = landed.shape[0]
    order_count = interp.shape[-1]
    level_count = interp.shape[1]
    coef_count = coeffs.shape[-1]
    first, second = coeffs.shape[2:4]
    u_count, v_count = src_span * first, tgt_span * second
    box_count = u_count * v_count
    square = order_count * order_count

    u_home = lax.axis_index("src")
    v_home = lax.axis_index("tgt")
    core = lax.axis_index("ill")
    home = u_home * tgt_span + v_home
    offsets = [(du, dv) for du in reversed(range(src_span)) for dv in reversed(range(tgt_span))]

    def device(k):
        return {
            "src": flipped("src", offsets[k][0]),
            "tgt": flipped("tgt", offsets[k][1]),
            "ill": 1 - core,
        }

    def place(k):
        return flipped("src", offsets[k][0]) * tgt_span + flipped("tgt", offsets[k][1])

    beside = [{"tgt": flipped("tgt", dv)} for dv in range(1, tgt_span)]
    partners = [device(k) for k in range(len(offsets))] + beside

    barrier = pltpu.get_barrier_semaphore()
    for partner in partners:
        pl.semaphore_signal(barrier, inc=1, device_id=partner, device_id_type=MESH)

    near = [
        pltpu.make_async_copy(orders_far, orders, near_sem.at[0]),
        pltpu.make_async_copy(reflection_far, reflection, near_sem.at[1]),
        pltpu.make_async_copy(interp_far, interp, near_sem.at[2]),
    ]
    for copy in near:
        copy.start()

    def out_copy(c, k):
        return pltpu.make_async_remote_copy(
            src_ref=coeffs.at[:, pl.ds(place(k) * chunks + c, 1)],
            dst_ref=landed.at[c, home],
            send_sem=send_sem.at[c, k],
            recv_sem=recv_sem.at[c, k],
            device_id=device(k),
            device_id_type=MESH,
        )

    def back_copy(c, k):
        return pltpu.make_async_remote_copy(
            src_ref=back.at[c, place(k)],
            dst_ref=out.at[:, pl.ds(home * chunks + c, 1)],
            send_sem=back_send_sem.at[c, k],
            recv_sem=back_recv_sem.at[c, k],
            device_id=device(k),
            device_id_type=MESH,
        )

    along = [device(k) for k, offset in enumerate(offsets) if offset[0] and not offset[1]]
    across = [device(k) for k, offset in enumerate(offsets) if not offset[0]] + beside

    def gather_copy(k):
        return pltpu.make_async_remote_copy(
            src_ref=mirror_out.at[core],
            dst_ref=mirror_in.at[core, v_home, u_home],
            send_sem=mirror_send_sem.at[k],
            recv_sem=mirror_recv_sem.at[k],
            device_id=along[k],
            device_id_type=MESH,
        )

    def share_copy(k):
        return pltpu.make_async_remote_copy(
            src_ref=mirror_in.at[1 - core, v_home],
            dst_ref=mirror_in.at[1 - core, v_home],
            send_sem=mirror_send_sem.at[len(along) + k],
            recv_sem=mirror_recv_sem.at[len(along) + k],
            device_id=across[k],
            device_id_type=MESH,
        )

    near[1].wait()
    mirror_out[...] = reflection[...].astype(jnp.bfloat16)
    mirror_in[1 - core, v_home, u_home] = mirror_out[1 - core]

    pl.semaphore_wait(barrier, len(partners))
    for k in range(len(along)):
        gather_copy(k).start()
    for k in range(len(offsets)):
        out_copy(0, k).start()
    for c in range(1, chunks):
        for k in range(len(offsets)):
            out_copy(c, k).start()

    near[0].wait()
    digits = (
        lax.div(orders[...], square),
        lax.rem(lax.div(orders[...], order_count), order_count),
        lax.rem(orders[...], order_count),
    )
    values = [
        jnp.cos(math.pi * (2.0 * d.astype(jnp.float32) + 1.0) / (2.0 * order_count))
        for d in digits
    ]

    def times(left, right):
        return (
            left[0] * right[0] - left[1] * right[1],
            left[0] * right[1] + left[1] * right[0],
        )

    def fill_phases(operator):
        direction = DIRECTIONS[operator]
        node = direction[0] * values[0] + direction[1] * values[1]
        node = node + direction[2] * values[2]
        turns = []
        for count, rate in ((u_count, PHASE_RATE), (v_count, PHASE_RATE * ALONG_SECOND)):
            position = lax.broadcasted_iota(jnp.int32, (count, coef_count), 0)
            angle = rate * (position.astype(jnp.float32) + 0.5) * node
            turns.append((jnp.cos(angle), jnp.sin(angle)))
        u_turn, v_turn = turns
        u_now, v_now = u_turn, v_turn
        for level in range(level_count):
            if level:
                u_now, v_now = times(u_now, u_turn), times(v_now, v_turn)
            n = operator * level_count + level
            outer, inner = (u_now, v_now) if n <= level_count else (v_now, u_now)
            span = inner[0].shape[0]
            for i in range(outer[0].shape[0]):
                turn = times((outer[0][i : i + 1], outer[1][i : i + 1]), inner)
                phase[n, 0, pl.ds(i * span, span), :] = turn[0]
                phase[n, 1, pl.ds(i * span, span), :] = turn[1]

    for operator in range(2):
        fill_phases(operator)

    column = lax.broadcasted_iota(jnp.int32, (order_count, coef_count), 1)
    point = lax.broadcasted_iota(jnp.int32, (order_count, coef_count), 0)
    column_digits = (
        lax.div(column, square),
        lax.rem(lax.div(column, order_count), order_count),
        lax.rem(column, order_count),
    )
    near[2].wait()
    for d in range(3):
        selector = (point == column_digits[d]).astype(jnp.float32)
        factors = interp[:, :, :, :, d].reshape(-1, order_count, order_count)
        factors = jnp.swapaxes(factors, 1, 2).reshape(-1, order_count)
        spread[d] = jnp.dot(
            factors, selector, precision=lax.Precision.HIGHEST,
            preferred_element_type=jnp.float32,
        )

    def build(index, carry):
        where = pl.ds(pl.multiple_of(index * order_count, order_count), order_count)
        n = lax.div(index, 4)
        side = lax.rem(lax.div(index, 2), 2)
        child = lax.rem(index, 2)
        columns = pl.ds(pl.multiple_of(side * coef_count, coef_count), coef_count)
        first_factor = spread[0, where, :]
        second_factor = spread[1, where, :]
        third_factor = spread[2, where, :]
        for a in range(order_count):
            pair = first_factor[a : a + 1, :] * second_factor
            block = pair[:, None, :] * third_factor[None, :, :]
            at = pl.multiple_of(child * coef_count + a * square, square)
            weight[n, pl.ds(at, square), columns] = block.reshape(square, coef_count).astype(
                jnp.bfloat16
            )
        return carry

    lax.fori_loop(0, 4 * level_count, build, 0)
    for k in range(len(along)):
        gather_copy(k).wait_recv()
    for k in range(len(across)):
        share_copy(k).start()
    lax.fori_loop(4 * level_count, 8 * level_count, build, 0)

    def modulate(blocks, table, n):
        result = [[], []]
        for i, (real, imag) in enumerate(zip(*blocks)):
            span = real.shape[0]
            at = pl.ds(i * span, span)
            new = times((table[n, 0, at, :], table[n, 1, at, :]), (real, imag))
            result[0].append(new[0])
            result[1].append(new[1])
        return result

    def apply_level(blocks, n, bit):
        count = len(blocks[0])
        low = [i for i in range(count) if not i >> bit & 1]
        parts = [
            jnp.concatenate([blocks[p][i + side * 2**bit] for p in range(2) for i in low], axis=0)
            for side in range(2)
        ]
        left = jnp.concatenate(parts, axis=1).astype(jnp.bfloat16)
        result = jnp.dot(left, weight[n], preferred_element_type=jnp.float32)
        new = [[None] * count, [None] * count]
        span = blocks[0][0].shape[0]
        for p in range(2):
            for at, i in enumerate(low):
                start = (p * len(low) + at) * span
                for side in range(2):
                    new[p][i + side * 2**bit] = result[
                        start : start + span, side * coef_count : (side + 1) * coef_count
                    ]
        return new

    def place_blocks(blocks):
        for p in range(2):
            for i, block in enumerate(blocks[p]):
                span = block.shape[0]
                lanes = rows.shape[-1]
                for g in range(rows.shape[0]):
                    rows[g, pl.ds(p * box_count + i * span, span), :] = block[
                        :, g * lanes : (g + 1) * lanes
                    ]

    def take(start, count, stride):
        return jnp.concatenate(
            [rows[g, pl.ds(start, count, stride), :] for g in range(rows.shape[0])], axis=1
        )

    def run(c):
        for k in range(len(offsets)):
            out_copy(c, k).wait_recv()
        lanes = rows.shape[-1]
        for p in range(2):
            for s in range(src_span):
                for t in range(tgt_span):
                    for i in range(first):
                        at = p * box_count + (s * first + i) * v_count + t * second
                        piece = landed[c, s * tgt_span + t, p, 0, i].astype(jnp.float32)
                        for g in range(rows.shape[0]):
                            rows[g, pl.ds(at, second), :] = piece[:, g * lanes : (g + 1) * lanes]
        blocks = [
            [take(p * box_count + i * v_count, v_count, 1) for i in range(u_count)]
            for p in range(2)
        ]
        u_top = u_count.bit_length() - 2
        v_top = v_count.bit_length() - 2
        for level in range(level_count):
            blocks = apply_level(modulate(blocks, phase, level), level, u_top - level)
        if c == 0:
            for k in range(len(across)):
                share_copy(k).wait_recv()
            for p in range(2):
                for s in range(src_span):
                    for t in range(tgt_span):
                        for i in range(first):
                            at = (s * first + i) * v_count + t * second
                            mirror[0, p, pl.ds(at, second), :] = mirror_in[
                                p, t, s, i
                            ].astype(jnp.float32)
            for i in range(u_count):
                at = pl.ds(i * v_count, v_count)
                both = times(
                    (mirror[0, 0, at, :], mirror[0, 1, at, :]),
                    (phase[level_count, 0, at, :], phase[level_count, 1, at, :]),
                )
                mirror[0, 0, at, :] = both[0]
                mirror[0, 1, at, :] = both[1]
        place_blocks(modulate(blocks, mirror, 0))
        blocks = [
            [take(p * box_count + i, u_count, v_count) for i in range(v_count)] for p in range(2)
        ]
        for level in range(level_count):
            n = level_count + level
            if level:
                blocks = modulate(blocks, phase, n)
            blocks = apply_level(blocks, n, v_top - level)
        place_blocks(blocks)
        for s in range(src_span):
            for t in range(tgt_span):
                for p in range(2):
                    for i in range(first):
                        at = p * box_count + t * second * u_count + s * first + i
                        back[c, s * tgt_span + t, p, 0, i] = take(at, second, u_count).astype(
                            jnp.bfloat16
                        )
        for k in range(len(offsets)):
            back_copy(c, k).start()

    for c in range(chunks):
        run(c)
    for k in range(len(offsets)):
        for c in range(chunks):
            out_copy(c, k).wait_send()
            back_copy(c, k).wait_recv()
            back_copy(c, k).wait_send()
    for k in range(len(along)):
        gather_copy(k).wait_send()
    for k in range(len(across)):
        share_copy(k).wait_send()


def by_spreading(coeffs, reflection, interp, orders):
    level_count = interp.shape[1]
    order_count = interp.shape[-1]
    _, ills, first, second, coef_count = coeffs.shape
    spans = (lax.axis_size("src"), lax.axis_size("tgt"))
    places = spans[0] * spans[1]
    chunks = ills // places
    box_count = places * first * second
    lanes = min(128, coef_count)
    far = pl.BlockSpec(memory_space=pltpu.HBM)
    operands = [
        pltpu.with_memory_space_constraint(operand, pltpu.HBM)
        for operand in (coeffs, reflection, interp, orders.reshape(1, coef_count))
    ]
    return pl.pallas_call(
        functools.partial(spread_kernel, spans),
        out_shape=jax.ShapeDtypeStruct(coeffs.shape, jnp.bfloat16),
        in_specs=[far] * 4,
        out_specs=pl.BlockSpec(memory_space=pltpu.VMEM),
        scratch_shapes=[
            pltpu.VMEM(reflection.shape, jnp.float32),
            pltpu.VMEM(interp.shape, jnp.float32),
            pltpu.VMEM((1, coef_count), jnp.int32),
            pltpu.VMEM((chunks, places, 2, 1, first, second, coef_count), jnp.bfloat16),
            pltpu.VMEM((chunks, places, 2, 1, first, second, coef_count), jnp.bfloat16),
            pltpu.VMEM(reflection.shape, jnp.bfloat16),
            pltpu.VMEM((2, spans[1], spans[0], first, second, coef_count), jnp.bfloat16),
            pltpu.VMEM((coef_count // lanes, 2 * box_count, lanes), jnp.float32),
            pltpu.VMEM((3, 8 * level_count * order_count, coef_count), jnp.float32),
            pltpu.VMEM((2 * level_count, 2, box_count, coef_count), jnp.float32),
            pltpu.VMEM((1, 2, box_count, coef_count), jnp.float32),
            pltpu.VMEM((2 * level_count, 2 * coef_count, 2 * coef_count), jnp.bfloat16),
            pltpu.SemaphoreType.DMA((3,)),
            pltpu.SemaphoreType.DMA((chunks, places)),
            pltpu.SemaphoreType.DMA((chunks, places)),
            pltpu.SemaphoreType.DMA((chunks, places)),
            pltpu.SemaphoreType.DMA((chunks, places)),
            pltpu.SemaphoreType.DMA((spans[0] + 2 * spans[1],)),
            pltpu.SemaphoreType.DMA((spans[0] + 2 * spans[1],)),
        ],
        compiler_params=pltpu.CompilerParams(
            collective_id=0, has_side_effects=True, vmem_limit_bytes=40 * 2**20
        ),
        name="butterfly",
    )(*operands)


def on_device(coeffs, reflection, interp, orders):
    level_count = interp.shape[1]
    _, ills, first, second, _ = coeffs.shape
    spans = (lax.axis_size("src"), lax.axis_size("tgt"))
    covers = spans[0] * first == 2**level_count and spans[1] * second == 2**level_count
    if covers and ills % (spans[0] * spans[1]) == 0 and lax.axis_size("ill") == 2:
        return by_spreading(coeffs, reflection, interp, orders)
    return by_swaps(coeffs, reflection, interp, orders)


def solution(mesh):
    in_specs = (
        P(None, ("groups", "ill"), "src", "tgt", None),
        P(None, ("groups", "src"), "tgt", None),
        P(),
        P(),
    )
    out_specs = P(None, ("groups", "ill"), "src", "tgt", None)
    return jax.shard_map(
        on_device, mesh=mesh, in_specs=in_specs, out_specs=out_specs, check_vma=False
    )
```

```python
import functools
import math

import jax
import jax.numpy as jnp
from jax import lax
from jax.experimental import pallas as pl
from jax.experimental.pallas import tpu as pltpu
from jax.sharding import PartitionSpec as P

PHASE_RATE = 0.3
ALONG_SECOND = 1.7
DIRECTIONS = ((0.6, 0.48, 0.64), (-0.36, 0.8, 0.48))
SHARES = (2, 4, 5, 5)
LEAD = 3
LAG = 2
FULL_ROWS = 128
MESH = pl.DeviceIdType.MESH


def level_plan(level_count, boxes, sizes):
    plan = []
    for operator, axis in enumerate(("src", "tgt")):
        local_bits = boxes[operator].bit_length() - 1
        top_bit = (boxes[operator] * sizes[operator]).bit_length() - 2
        row_span = boxes[1] if operator == 0 else 1
        for level in range(level_count):
            bit = top_bit - level
            if bit >= local_bits:
                plan.append((operator, level, axis, 2 ** (bit - local_bits)))
            else:
                plan.append((operator, level, None, row_span * 2**bit))
    return plan


def own_bit(axis, mask):
    return lax.rem(lax.div(lax.axis_index(axis), mask), 2)


def partner_of(axis, mask):
    return lax.axis_index(axis) + mask * (1 - 2 * own_bit(axis, mask))


def swap_kernel(
    plan,
    boxes,
    sizes,
    coeffs,
    reflection_far,
    interp_far,
    orders_far,
    out,
    own,
    reflection,
    interp,
    orders,
    landed,
    held,
    sent,
    total,
    rows,
    spread,
    phase,
    weight,
    mirror,
    own_sem,
    send_sem,
    recv_sem,
):
    order_count = interp.shape[-1]
    coef_count = coeffs.shape[-1]
    first, second = boxes
    tile = first * second
    chunks = len(sizes)
    starts = [sum(sizes[:c]) for c in range(chunks)]
    swaps = [n for n, item in enumerate(plan) if item[2] is not None]

    def chunk(c):
        return pl.ds(2 * tile * starts[c], 2 * tile * sizes[c])

    barrier = pltpu.get_barrier_semaphore()
    for n in swaps:
        axis, mask = plan[n][2:]
        pl.semaphore_signal(
            barrier, inc=1, device_id={axis: partner_of(axis, mask)}, device_id_type=MESH
        )
    pl.semaphore_wait(barrier, len(swaps))

    def raw_copy(c):
        axis, mask = plan[0][2:]
        return pltpu.make_async_remote_copy(
            src_ref=coeffs.at[:, pl.ds(starts[c], sizes[c])],
            dst_ref=landed.at[:, pl.ds(starts[c], sizes[c])],
            send_sem=send_sem.at[0, c],
            recv_sem=recv_sem.at[0, c],
            device_id={axis: partner_of(axis, mask)},
            device_id_type=MESH,
        )

    def state_copy(s, c):
        axis, mask = plan[swaps[s]][2:]
        return pltpu.make_async_remote_copy(
            src_ref=sent.at[s - 1, chunk(c)],
            dst_ref=held.at[s - 1, chunk(c)],
            send_sem=send_sem.at[s, c],
            recv_sem=recv_sem.at[s, c],
            device_id={axis: partner_of(axis, mask)},
            device_id_type=MESH,
        )

    lead = min(LEAD, chunks) if len(swaps) > 1 else chunks
    for c in range(lead):
        raw_copy(c).start()
    own_copy = pltpu.make_async_copy(coeffs, own, own_sem.at[0])
    near = [
        pltpu.make_async_copy(orders_far, orders, own_sem.at[1]),
        pltpu.make_async_copy(interp_far, interp, own_sem.at[2]),
        pltpu.make_async_copy(reflection_far, reflection, own_sem.at[3]),
    ]
    for copy in near:
        copy.start()
    own_copy.start()
    near[0].wait()

    digits = (
        lax.div(orders[...], order_count * order_count),
        lax.rem(lax.div(orders[...], order_count), order_count),
        lax.rem(orders[...], order_count),
    )
    values = [
        jnp.cos(math.pi * (2.0 * d.astype(jnp.float32) + 1.0) / (2.0 * order_count))
        for d in digits
    ]
    products = []
    for direction in DIRECTIONS:
        summed = direction[0] * values[0] + direction[1] * values[1]
        products.append(summed + direction[2] * values[2])
    row = lax.broadcasted_iota(jnp.int32, (tile, coef_count), 0)

    def fill_phase(slot, operator, level, u_start, v_start):
        u = (lax.div(row, second) + u_start).astype(jnp.float32)
        v = (lax.rem(row, second) + v_start).astype(jnp.float32)
        position = (u + 0.5) + ALONG_SECOND * (v + 0.5)
        angle = (PHASE_RATE * (level + 1)) * position * products[operator]
        phase[slot, 0] = jnp.cos(angle).astype(jnp.bfloat16).astype(jnp.float32)
        phase[slot, 1] = jnp.sin(angle).astype(jnp.bfloat16).astype(jnp.float32)

    u_own = lax.axis_index("src") * first
    v_own = lax.axis_index("tgt") * second
    fill_phase(0, plan[0][0], plan[0][1], u_own, v_own)

    column = lax.broadcasted_iota(jnp.int32, (order_count, coef_count), 1)
    point = lax.broadcasted_iota(jnp.int32, (order_count, coef_count), 0)
    column_digits = (
        lax.div(column, order_count * order_count),
        lax.rem(lax.div(column, order_count), order_count),
        lax.rem(column, order_count),
    )
    near[1].wait()
    for d in range(3):
        selector = (point == column_digits[d]).astype(jnp.float32)
        factors = interp[:, :, :, :, d].reshape(-1, order_count, order_count)
        factors = jnp.swapaxes(factors, 1, 2).reshape(-1, order_count)
        spread[d] = jnp.dot(
            factors, selector, precision=lax.Precision.HIGHEST,
            preferred_element_type=jnp.float32,
        )

    square = order_count * order_count

    def build(slot, index):
        where = pl.ds(pl.multiple_of(index * order_count, order_count), order_count)
        first_factor = spread[0, where, :]
        second_factor = spread[1, where, :]
        third_factor = spread[2, where, :]
        for a in range(order_count):
            pair = first_factor[a : a + 1, :] * second_factor
            block = pair[:, None, :] * third_factor[None, :, :]
            weight[slot, pl.ds(a * square, square), :] = block.reshape(
                square, coef_count
            ).astype(jnp.bfloat16)

    level_count = interp.shape[1]
    slots = []
    used = 0
    for item in plan:
        slots.append(used)
        used += 2 if item[2] is not None else 4

    def build_level(n):
        operator, level, axis, mask = plan[n]
        base = (operator * level_count + level) * 4
        if axis is None:
            def step(j, carry):
                build(slots[n] + j, base + j)
                return carry
            lax.fori_loop(0, 4, step, 0)
        else:
            bit = own_bit(axis, mask)

            def step(j, carry):
                child = bit + j - 2 * bit * j
                build(slots[n] + j, base + 2 * bit + child)
                return carry
            lax.fori_loop(0, 2, step, 0)

    def dot(left, slot):
        return jnp.dot(left, weight[slot], preferred_element_type=jnp.float32)

    def modulate(value, cos_part, sin_part):
        half = value.shape[0] // 2
        shape = (half // tile, tile, coef_count)
        real = value[:half].reshape(shape)
        imag = value[half:].reshape(shape)
        new_real = cos_part * real - sin_part * imag
        new_imag = cos_part * imag + sin_part * real
        return jnp.concatenate(
            [new_real.reshape(half, coef_count), new_imag.reshape(half, coef_count)], axis=0
        ).astype(jnp.bfloat16)

    def gather_rows(ref, c):
        for p in range(2):
            for i in range(sizes[c]):
                for u in range(first):
                    at = (p * sizes[c] + i) * tile + u * second
                    rows[pl.ds(at, second), :] = ref[p, starts[c] + i, u].astype(jnp.float32)
        return rows[: 2 * sizes[c] * tile, :]

    build_level(0)
    own_copy.wait()

    for c in range(chunks):
        moved = modulate(gather_rows(own, c), phase[0, 0], phase[0, 1])
        total[0, chunk(c), :] = dot(moved, slots[0])

    axis, mask = plan[0][2:]
    shift = (partner_of(axis, mask) - lax.axis_index(axis)) * (
        first if axis == "src" else second
    )
    fill_phase(
        len(plan),
        plan[0][0],
        plan[0][1],
        u_own + (shift if axis == "src" else 0),
        v_own + (shift if axis == "tgt" else 0),
    )
    ends = [0] + swaps[1:] + [len(plan) - 1]

    def prepare(s):
        for n in range(ends[s] + 1, ends[s + 1] + 1):
            fill_phase(n, plan[n][0], plan[n][1], u_own, v_own)
            build_level(n)

    prepare(0)
    near[2].wait()
    for p in range(2):
        for u in range(first):
            mirror[p, pl.ds(u * second, second), :] = reflection[p, u]

    def stage(s, c):
        n = swaps[s]
        if s == 0:
            raw_copy(c).wait_recv()
            value = gather_rows(landed, c)
            received = modulate(value, phase[len(plan), 0], phase[len(plan), 1])
        else:
            state_copy(s, c).wait_recv()
            received = held[s - 1, chunk(c), :]
        chunk_rows = 2 * tile * sizes[c]
        row_index = lax.broadcasted_iota(jnp.int32, (chunk_rows, coef_count), 0)
        summed = total[s, chunk(c), :] + dot(received, slots[n] + 1)
        state = summed.astype(jnp.bfloat16).astype(jnp.float32)
        last = swaps[s + 1] if s + 1 < len(swaps) else len(plan)
        for m in range(n + 1, last + 1):
            before = plan[m - 1][0]
            if before == 0 and (m == len(plan) or plan[m][0] == 1):
                state = (
                    modulate(state, mirror[0], mirror[1]).astype(jnp.float32)
                )
            if m == len(plan):
                break
            moved = modulate(state, phase[m, 0], phase[m, 1])
            if m == last:
                sent[s, chunk(c), :] = moved
                state_copy(s + 1, c).start()
                if s == 0 and c + lead < chunks:
                    raw_copy(c + lead).start()
                total[s + 1, chunk(c), :] = dot(moved, slots[m])
                return
            span = plan[m][3]
            upper_row = lax.rem(lax.div(row_index, span), 2) == 1
            wide = moved.astype(jnp.float32)
            lower = jnp.where(upper_row, pltpu.roll(wide, span, 0), wide).astype(jnp.bfloat16)
            upper = jnp.where(
                upper_row, wide, pltpu.roll(wide, chunk_rows - span, 0)
            ).astype(jnp.bfloat16)
            low = dot(lower, slots[m]) + dot(upper, slots[m] + 1)
            high = dot(lower, slots[m] + 2) + dot(upper, slots[m] + 3)
            state = jnp.where(upper_row, high, low).astype(jnp.bfloat16).astype(jnp.float32)
        result = state.astype(jnp.bfloat16).reshape(2, sizes[c], tile, coef_count)
        out[:, pl.ds(starts[c], sizes[c])] = result

    for t in range(chunks + LAG * (len(swaps) - 1)):
        for s in range(len(swaps)):
            if 0 <= t - LAG * s < chunks:
                stage(s, t - LAG * s)
        if 1 <= t + 1 < len(swaps):
            prepare(t + 1)

    for c in range(chunks):
        raw_copy(c).wait_send()
        for s in range(1, len(swaps)):
            state_copy(s, c).wait_send()


def by_swaps(coeffs, reflection, interp, orders):
    level_count = interp.shape[1]
    order_count = interp.shape[-1]
    _, ills, first, second, coef_count = coeffs.shape
    sizes_of = [ills * share // sum(SHARES) for share in SHARES]
    sizes_of[0] += ills - sum(sizes_of)
    sizes_of = [size for size in sizes_of if size > 0]
    chunks = len(sizes_of)
    tile = first * second
    sizes = (lax.axis_size("src"), lax.axis_size("tgt"))
    plan = level_plan(level_count, (first, second), sizes)
    swap_count = sum(item[2] is not None for item in plan)
    slot_count = 2 * swap_count + 4 * (len(plan) - swap_count)
    state_rows = 2 * ills * tile
    later = max(swap_count - 1, 1)
    whole = pl.BlockSpec(memory_space=pltpu.VMEM)
    result = pl.pallas_call(
        functools.partial(swap_kernel, plan, (first, second), sizes_of),
        out_shape=jax.ShapeDtypeStruct((2, ills, tile, coef_count), jnp.bfloat16),
        in_specs=[pl.BlockSpec(memory_space=pl.ANY)] * 4,
        out_specs=whole,
        scratch_shapes=[
            pltpu.VMEM(coeffs.shape, jnp.bfloat16),
            pltpu.VMEM(reflection.shape, jnp.float32),
            pltpu.VMEM(interp.shape, jnp.float32),
            pltpu.VMEM((1, coef_count), jnp.int32),
            pltpu.VMEM(coeffs.shape, jnp.bfloat16),
            pltpu.VMEM((later, state_rows, coef_count), jnp.bfloat16),
            pltpu.VMEM((later, state_rows, coef_count), jnp.bfloat16),
            pltpu.VMEM((swap_count, state_rows, coef_count), jnp.float32),
            pltpu.VMEM((2 * tile * max(sizes_of), coef_count), jnp.float32),
            pltpu.VMEM((3, 8 * level_count * order_count, coef_count), jnp.float32),
            pltpu.VMEM((len(plan) + 1, 2, tile, coef_count), jnp.float32),
            pltpu.VMEM((slot_count, coef_count, coef_count), jnp.bfloat16),
            pltpu.VMEM((2, tile, coef_count), jnp.float32),
            pltpu.SemaphoreType.DMA((4,)),
            pltpu.SemaphoreType.DMA((swap_count, chunks)),
            pltpu.SemaphoreType.DMA((swap_count, chunks)),
        ],
        compiler_params=pltpu.CompilerParams(
            collective_id=0, has_side_effects=True, vmem_limit_bytes=60 * 2**20
        ),
        name="butterfly",
    )(coeffs, reflection, interp, orders.reshape(1, coef_count))
    return result.reshape(coeffs.shape)


def flipped(axis, mask):
    index = lax.axis_index(axis)
    for bit in range(mask.bit_length()):
        if mask >> bit & 1:
            index = index + 2**bit * (1 - 2 * lax.rem(lax.div(index, 2**bit), 2))
    return index


def spread_kernel(
    spans,
    coeffs,
    reflection_far,
    interp_far,
    orders_far,
    out,
    reflection,
    interp,
    orders,
    landed,
    back,
    mirror_out,
    mirror_in,
    rows,
    spread,
    phase,
    mirror,
    weight,
    near_sem,
    send_sem,
    recv_sem,
    back_send_sem,
    back_recv_sem,
    gather_send_sem,
    gather_recv_sem,
    share_send_sem,
    share_recv_sem,
):
    src_span, tgt_span = spans
    chunks = landed.shape[0]
    order_count = interp.shape[-1]
    level_count = interp.shape[1]
    coef_count = coeffs.shape[-1]
    first, second = coeffs.shape[2:4]
    u_count, v_count = src_span * first, tgt_span * second
    box_count = u_count * v_count
    square = order_count * order_count

    u_home = lax.axis_index("src")
    v_home = lax.axis_index("tgt")
    core = lax.axis_index("ill")
    home = u_home * tgt_span + v_home
    offsets = [(du, dv) for du in reversed(range(src_span)) for dv in reversed(range(tgt_span))]

    def device(k):
        return {
            "src": flipped("src", offsets[k][0]),
            "tgt": flipped("tgt", offsets[k][1]),
            "ill": 1 - core,
        }

    def place(k):
        return flipped("src", offsets[k][0]) * tgt_span + flipped("tgt", offsets[k][1])

    beside = [{"tgt": flipped("tgt", dv)} for dv in range(1, tgt_span)]
    partners = [device(k) for k in range(len(offsets))] + beside

    barrier = pltpu.get_barrier_semaphore()
    for partner in partners:
        pl.semaphore_signal(barrier, inc=1, device_id=partner, device_id_type=MESH)

    near = [
        pltpu.make_async_copy(orders_far, orders, near_sem.at[0]),
        pltpu.make_async_copy(reflection_far, reflection, near_sem.at[1]),
        pltpu.make_async_copy(interp_far, interp, near_sem.at[2]),
    ]
    for copy in near:
        copy.start()

    def out_copy(c, k):
        return pltpu.make_async_remote_copy(
            src_ref=coeffs.at[:, pl.ds(place(k) * chunks + c, 1)],
            dst_ref=landed.at[c, home],
            send_sem=send_sem.at[c, k],
            recv_sem=recv_sem.at[c, k],
            device_id=device(k),
            device_id_type=MESH,
        )

    def back_copy(c, k):
        return pltpu.make_async_remote_copy(
            src_ref=back.at[c, place(k)],
            dst_ref=out.at[:, pl.ds(home * chunks + c, 1)],
            send_sem=back_send_sem.at[c, k],
            recv_sem=back_recv_sem.at[c, k],
            device_id=device(k),
            device_id_type=MESH,
        )

    across = [device(k) for k, offset in enumerate(offsets) if not offset[0]] + beside

    def gather_copy(du):
        return pltpu.make_async_remote_copy(
            src_ref=mirror_out.at[core],
            dst_ref=mirror_in.at[core, v_home, u_home],
            send_sem=gather_send_sem.at[du],
            recv_sem=gather_recv_sem.at[du],
            device_id=device(offsets.index((du, 0))),
            device_id_type=MESH,
        )

    def share_copy(du, k):
        block = mirror_in.at[1 - core, v_home, flipped("src", du)]
        return pltpu.make_async_remote_copy(
            src_ref=block,
            dst_ref=block,
            send_sem=share_send_sem.at[du, k],
            recv_sem=share_recv_sem.at[du, k],
            device_id=across[k],
            device_id_type=MESH,
        )

    def share(du):
        if du:
            gather_copy(du).wait_recv()
        for k in range(len(across)):
            share_copy(du, k).start()

    near[1].wait()
    mirror_out[...] = reflection[...].astype(jnp.bfloat16)
    mirror_in[1 - core, v_home, u_home] = mirror_out[1 - core]

    pl.semaphore_wait(barrier, len(partners))
    for du in reversed(range(1, src_span)):
        gather_copy(du).start()
    share(0)
    for k in range(len(offsets)):
        out_copy(0, k).start()
    for c in range(1, chunks):
        for k in range(len(offsets)):
            out_copy(c, k).start()

    near[0].wait()
    digits = (
        lax.div(orders[...], square),
        lax.rem(lax.div(orders[...], order_count), order_count),
        lax.rem(orders[...], order_count),
    )
    values = [
        jnp.cos(math.pi * (2.0 * d.astype(jnp.float32) + 1.0) / (2.0 * order_count))
        for d in digits
    ]

    def times(left, right):
        return (
            left[0] * right[0] - left[1] * right[1],
            left[0] * right[1] + left[1] * right[0],
        )

    def fill_phases(operator):
        direction = DIRECTIONS[operator]
        node = direction[0] * values[0] + direction[1] * values[1]
        node = node + direction[2] * values[2]
        turns = []
        for count, rate in ((u_count, PHASE_RATE), (v_count, PHASE_RATE * ALONG_SECOND)):
            position = lax.broadcasted_iota(jnp.int32, (count, coef_count), 0)
            angle = rate * (position.astype(jnp.float32) + 0.5) * node
            turns.append((jnp.cos(angle), jnp.sin(angle)))
        u_turn, v_turn = turns
        u_now, v_now = u_turn, v_turn
        for level in range(level_count):
            if level:
                u_now, v_now = times(u_now, u_turn), times(v_now, v_turn)
            n = operator * level_count + level
            outer, inner = (u_now, v_now) if n <= level_count else (v_now, u_now)
            span = inner[0].shape[0]
            for i in range(outer[0].shape[0]):
                turn = times((outer[0][i : i + 1], outer[1][i : i + 1]), inner)
                phase[n, 0, pl.ds(i * span, span), :] = turn[0]
                phase[n, 1, pl.ds(i * span, span), :] = turn[1]

    for operator in range(2):
        fill_phases(operator)

    column = lax.broadcasted_iota(jnp.int32, (order_count, coef_count), 1)
    point = lax.broadcasted_iota(jnp.int32, (order_count, coef_count), 0)
    column_digits = (
        lax.div(column, square),
        lax.rem(lax.div(column, order_count), order_count),
        lax.rem(column, order_count),
    )
    near[2].wait()
    for d in range(3):
        selector = (point == column_digits[d]).astype(jnp.float32)
        factors = interp[:, :, :, :, d].reshape(-1, order_count, order_count)
        factors = jnp.swapaxes(factors, 1, 2).reshape(-1, order_count)
        spread[d] = jnp.dot(
            factors, selector, precision=lax.Precision.HIGHEST,
            preferred_element_type=jnp.float32,
        )

    def build(index, carry):
        where = pl.ds(pl.multiple_of(index * order_count, order_count), order_count)
        n = lax.div(index, 4)
        side = lax.rem(lax.div(index, 2), 2)
        child = lax.rem(index, 2)
        columns = pl.ds(pl.multiple_of(side * coef_count, coef_count), coef_count)
        first_factor = spread[0, where, :]
        second_factor = spread[1, where, :]
        third_factor = spread[2, where, :]
        for a in range(order_count):
            pair = first_factor[a : a + 1, :] * second_factor
            block = pair[:, None, :] * third_factor[None, :, :]
            at = pl.multiple_of(child * coef_count + a * square, square)
            weight[n, pl.ds(at, square), columns] = block.reshape(square, coef_count).astype(
                jnp.bfloat16
            )
        return carry

    marks = (0, 4 * level_count, 4 * level_count, 8 * level_count)
    lax.fori_loop(marks[0], marks[1], build, 0)
    for du in range(1, src_span - 1):
        share(du)
    lax.fori_loop(marks[1], marks[2], build, 0)
    if src_span > 1:
        share(src_span - 1)
    lax.fori_loop(marks[2], marks[3], build, 0)

    def modulate(blocks, table, n):
        result = [[], []]
        for i, (real, imag) in enumerate(zip(*blocks)):
            span = real.shape[0]
            at = pl.ds(i * span, span)
            new = times((table[n, 0, at, :], table[n, 1, at, :]), (real, imag))
            result[0].append(new[0])
            result[1].append(new[1])
        return result

    def apply_level(blocks, n, bit):
        count = len(blocks[0])
        low = [i for i in range(count) if not i >> bit & 1]
        parts = [
            jnp.concatenate([blocks[p][i + side * 2**bit] for p in range(2) for i in low], axis=0)
            for side in range(2)
        ]
        left = jnp.concatenate(parts, axis=1).astype(jnp.bfloat16)
        left = jnp.concatenate([left] * max(1, FULL_ROWS // left.shape[0]), axis=0)
        result = jnp.dot(left, weight[n], preferred_element_type=jnp.float32)
        new = [[None] * count, [None] * count]
        span = blocks[0][0].shape[0]
        for p in range(2):
            for at, i in enumerate(low):
                start = (p * len(low) + at) * span
                for side in range(2):
                    new[p][i + side * 2**bit] = result[
                        start : start + span, side * coef_count : (side + 1) * coef_count
                    ]
        return new

    def place_blocks(blocks):
        for p in range(2):
            for i, block in enumerate(blocks[p]):
                span = block.shape[0]
                lanes = rows.shape[-1]
                for g in range(rows.shape[0]):
                    rows[g, pl.ds(p * box_count + i * span, span), :] = block[
                        :, g * lanes : (g + 1) * lanes
                    ]

    def take(start, count, stride):
        return jnp.concatenate(
            [rows[g, pl.ds(start, count, stride), :] for g in range(rows.shape[0])], axis=1
        )

    def run(c):
        for k in range(len(offsets)):
            out_copy(c, k).wait_recv()
        lanes = rows.shape[-1]
        for p in range(2):
            for s in range(src_span):
                for t in range(tgt_span):
                    for i in range(first):
                        at = p * box_count + (s * first + i) * v_count + t * second
                        piece = landed[c, s * tgt_span + t, p, 0, i].astype(jnp.float32)
                        for g in range(rows.shape[0]):
                            rows[g, pl.ds(at, second), :] = piece[:, g * lanes : (g + 1) * lanes]
        blocks = [
            [take(p * box_count + i * v_count, v_count, 1) for i in range(u_count)]
            for p in range(2)
        ]
        u_top = u_count.bit_length() - 2
        v_top = v_count.bit_length() - 2
        for level in range(level_count):
            blocks = apply_level(modulate(blocks, phase, level), level, u_top - level)
        if c == 0:
            for du in range(src_span):
                for k in range(len(across)):
                    share_copy(du, k).wait_recv()
            for p in range(2):
                for s in range(src_span):
                    for t in range(tgt_span):
                        for i in range(first):
                            at = (s * first + i) * v_count + t * second
                            mirror[0, p, pl.ds(at, second), :] = mirror_in[
                                p, t, s, i
                            ].astype(jnp.float32)
            for i in range(u_count):
                at = pl.ds(i * v_count, v_count)
                both = times(
                    (mirror[0, 0, at, :], mirror[0, 1, at, :]),
                    (phase[level_count, 0, at, :], phase[level_count, 1, at, :]),
                )
                mirror[0, 0, at, :] = both[0]
                mirror[0, 1, at, :] = both[1]
        place_blocks(modulate(blocks, mirror, 0))
        blocks = [
            [take(p * box_count + i, u_count, v_count) for i in range(v_count)] for p in range(2)
        ]
        for level in range(level_count):
            n = level_count + level
            if level:
                blocks = modulate(blocks, phase, n)
            blocks = apply_level(blocks, n, v_top - level)
        place_blocks(blocks)
        for s in range(src_span):
            for t in range(tgt_span):
                for p in range(2):
                    for i in range(first):
                        at = p * box_count + t * second * u_count + s * first + i
                        back[c, s * tgt_span + t, p, 0, i] = take(at, second, u_count).astype(
                            jnp.bfloat16
                        )
        for k in range(len(offsets)):
            back_copy(c, k).start()

    for c in range(chunks):
        run(c)
    for k in range(len(offsets)):
        for c in range(chunks):
            out_copy(c, k).wait_send()
            back_copy(c, k).wait_recv()
            back_copy(c, k).wait_send()
    for du in range(src_span):
        if du:
            gather_copy(du).wait_send()
        for k in range(len(across)):
            share_copy(du, k).wait_send()


def by_spreading(coeffs, reflection, interp, orders):
    level_count = interp.shape[1]
    order_count = interp.shape[-1]
    _, ills, first, second, coef_count = coeffs.shape
    spans = (lax.axis_size("src"), lax.axis_size("tgt"))
    places = spans[0] * spans[1]
    chunks = ills // places
    box_count = places * first * second
    lanes = min(128, coef_count)
    far = pl.BlockSpec(memory_space=pltpu.HBM)
    operands = [
        pltpu.with_memory_space_constraint(operand, pltpu.HBM)
        for operand in (coeffs, reflection, interp, orders.reshape(1, coef_count))
    ]
    return pl.pallas_call(
        functools.partial(spread_kernel, spans),
        out_shape=jax.ShapeDtypeStruct(coeffs.shape, jnp.bfloat16),
        in_specs=[far] * 4,
        out_specs=pl.BlockSpec(memory_space=pltpu.VMEM),
        scratch_shapes=[
            pltpu.VMEM(reflection.shape, jnp.float32),
            pltpu.VMEM(interp.shape, jnp.float32),
            pltpu.VMEM((1, coef_count), jnp.int32),
            pltpu.VMEM((chunks, places, 2, 1, first, second, coef_count), jnp.bfloat16),
            pltpu.VMEM((chunks, places, 2, 1, first, second, coef_count), jnp.bfloat16),
            pltpu.VMEM(reflection.shape, jnp.bfloat16),
            pltpu.VMEM((2, spans[1], spans[0], first, second, coef_count), jnp.bfloat16),
            pltpu.VMEM((coef_count // lanes, 2 * box_count, lanes), jnp.float32),
            pltpu.VMEM((3, 8 * level_count * order_count, coef_count), jnp.float32),
            pltpu.VMEM((2 * level_count, 2, box_count, coef_count), jnp.float32),
            pltpu.VMEM((1, 2, box_count, coef_count), jnp.float32),
            pltpu.VMEM((2 * level_count, 2 * coef_count, 2 * coef_count), jnp.bfloat16),
            pltpu.SemaphoreType.DMA((3,)),
            pltpu.SemaphoreType.DMA((chunks, places)),
            pltpu.SemaphoreType.DMA((chunks, places)),
            pltpu.SemaphoreType.DMA((chunks, places)),
            pltpu.SemaphoreType.DMA((chunks, places)),
            pltpu.SemaphoreType.DMA((spans[0],)),
            pltpu.SemaphoreType.DMA((spans[0],)),
            pltpu.SemaphoreType.DMA((spans[0], 2 * spans[1])),
            pltpu.SemaphoreType.DMA((spans[0], 2 * spans[1])),
        ],
        compiler_params=pltpu.CompilerParams(
            collective_id=0, has_side_effects=True, vmem_limit_bytes=40 * 2**20
        ),
        name="butterfly",
    )(*operands)


def on_device(coeffs, reflection, interp, orders):
    level_count = interp.shape[1]
    _, ills, first, second, _ = coeffs.shape
    spans = (lax.axis_size("src"), lax.axis_size("tgt"))
    covers = spans[0] * first == 2**level_count and spans[1] * second == 2**level_count
    if covers and ills % (spans[0] * spans[1]) == 0 and lax.axis_size("ill") == 2:
        return by_spreading(coeffs, reflection, interp, orders)
    return by_swaps(coeffs, reflection, interp, orders)


def solution(mesh):
    in_specs = (
        P(None, ("groups", "ill"), "src", "tgt", None),
        P(None, ("groups", "src"), "tgt", None),
        P(),
        P(),
    )
    out_specs = P(None, ("groups", "ill"), "src", "tgt", None)
    return jax.shard_map(
        on_device, mesh=mesh, in_specs=in_specs, out_specs=out_specs, check_vma=False
    )
```

```python
import functools
import math

import jax
import jax.numpy as jnp
from jax import lax
from jax.experimental import pallas as pl
from jax.experimental.pallas import tpu as pltpu
from jax.sharding import PartitionSpec as P

PHASE_RATE = 0.3
ALONG_SECOND = 1.7
DIRECTIONS = ((0.6, 0.48, 0.64), (-0.36, 0.8, 0.48))
SHARES = (2, 4, 5, 5)
LEAD = 3
LAG = 2
FULL_ROWS = 128
MESH = pl.DeviceIdType.MESH


def level_plan(level_count, boxes, sizes):
    plan = []
    for operator, axis in enumerate(("src", "tgt")):
        local_bits = boxes[operator].bit_length() - 1
        top_bit = (boxes[operator] * sizes[operator]).bit_length() - 2
        row_span = boxes[1] if operator == 0 else 1
        for level in range(level_count):
            bit = top_bit - level
            if bit >= local_bits:
                plan.append((operator, level, axis, 2 ** (bit - local_bits)))
            else:
                plan.append((operator, level, None, row_span * 2**bit))
    return plan


def own_bit(axis, mask):
    return lax.rem(lax.div(lax.axis_index(axis), mask), 2)


def partner_of(axis, mask):
    return lax.axis_index(axis) + mask * (1 - 2 * own_bit(axis, mask))


def swap_kernel(
    plan,
    boxes,
    sizes,
    coeffs,
    reflection_far,
    interp_far,
    orders_far,
    out,
    own,
    reflection,
    interp,
    orders,
    landed,
    held,
    sent,
    total,
    rows,
    spread,
    phase,
    weight,
    mirror,
    own_sem,
    send_sem,
    recv_sem,
):
    order_count = interp.shape[-1]
    coef_count = coeffs.shape[-1]
    first, second = boxes
    tile = first * second
    chunks = len(sizes)
    starts = [sum(sizes[:c]) for c in range(chunks)]
    swaps = [n for n, item in enumerate(plan) if item[2] is not None]

    def chunk(c):
        return pl.ds(2 * tile * starts[c], 2 * tile * sizes[c])

    barrier = pltpu.get_barrier_semaphore()
    for n in swaps:
        axis, mask = plan[n][2:]
        pl.semaphore_signal(
            barrier, inc=1, device_id={axis: partner_of(axis, mask)}, device_id_type=MESH
        )
    pl.semaphore_wait(barrier, len(swaps))

    def raw_copy(c):
        axis, mask = plan[0][2:]
        return pltpu.make_async_remote_copy(
            src_ref=coeffs.at[:, pl.ds(starts[c], sizes[c])],
            dst_ref=landed.at[:, pl.ds(starts[c], sizes[c])],
            send_sem=send_sem.at[0, c],
            recv_sem=recv_sem.at[0, c],
            device_id={axis: partner_of(axis, mask)},
            device_id_type=MESH,
        )

    def state_copy(s, c):
        axis, mask = plan[swaps[s]][2:]
        return pltpu.make_async_remote_copy(
            src_ref=sent.at[s - 1, chunk(c)],
            dst_ref=held.at[s - 1, chunk(c)],
            send_sem=send_sem.at[s, c],
            recv_sem=recv_sem.at[s, c],
            device_id={axis: partner_of(axis, mask)},
            device_id_type=MESH,
        )

    lead = min(LEAD, chunks) if len(swaps) > 1 else chunks
    for c in range(lead):
        raw_copy(c).start()
    own_copy = pltpu.make_async_copy(coeffs, own, own_sem.at[0])
    near = [
        pltpu.make_async_copy(orders_far, orders, own_sem.at[1]),
        pltpu.make_async_copy(interp_far, interp, own_sem.at[2]),
        pltpu.make_async_copy(reflection_far, reflection, own_sem.at[3]),
    ]
    for copy in near:
        copy.start()
    own_copy.start()
    near[0].wait()

    digits = (
        lax.div(orders[...], order_count * order_count),
        lax.rem(lax.div(orders[...], order_count), order_count),
        lax.rem(orders[...], order_count),
    )
    values = [
        jnp.cos(math.pi * (2.0 * d.astype(jnp.float32) + 1.0) / (2.0 * order_count))
        for d in digits
    ]
    products = []
    for direction in DIRECTIONS:
        summed = direction[0] * values[0] + direction[1] * values[1]
        products.append(summed + direction[2] * values[2])
    row = lax.broadcasted_iota(jnp.int32, (tile, coef_count), 0)

    def fill_phase(slot, operator, level, u_start, v_start):
        u = (lax.div(row, second) + u_start).astype(jnp.float32)
        v = (lax.rem(row, second) + v_start).astype(jnp.float32)
        position = (u + 0.5) + ALONG_SECOND * (v + 0.5)
        angle = (PHASE_RATE * (level + 1)) * position * products[operator]
        phase[slot, 0] = jnp.cos(angle).astype(jnp.bfloat16).astype(jnp.float32)
        phase[slot, 1] = jnp.sin(angle).astype(jnp.bfloat16).astype(jnp.float32)

    u_own = lax.axis_index("src") * first
    v_own = lax.axis_index("tgt") * second
    fill_phase(0, plan[0][0], plan[0][1], u_own, v_own)

    column = lax.broadcasted_iota(jnp.int32, (order_count, coef_count), 1)
    point = lax.broadcasted_iota(jnp.int32, (order_count, coef_count), 0)
    column_digits = (
        lax.div(column, order_count * order_count),
        lax.rem(lax.div(column, order_count), order_count),
        lax.rem(column, order_count),
    )
    near[1].wait()
    for d in range(3):
        selector = (point == column_digits[d]).astype(jnp.float32)
        factors = interp[:, :, :, :, d].reshape(-1, order_count, order_count)
        factors = jnp.swapaxes(factors, 1, 2).reshape(-1, order_count)
        spread[d] = jnp.dot(
            factors, selector, precision=lax.Precision.HIGHEST,
            preferred_element_type=jnp.float32,
        )

    square = order_count * order_count

    def build(slot, index):
        where = pl.ds(pl.multiple_of(index * order_count, order_count), order_count)
        first_factor = spread[0, where, :]
        second_factor = spread[1, where, :]
        third_factor = spread[2, where, :]
        for a in range(order_count):
            pair = first_factor[a : a + 1, :] * second_factor
            block = pair[:, None, :] * third_factor[None, :, :]
            weight[slot, pl.ds(a * square, square), :] = block.reshape(
                square, coef_count
            ).astype(jnp.bfloat16)

    level_count = interp.shape[1]
    slots = []
    used = 0
    for item in plan:
        slots.append(used)
        used += 2 if item[2] is not None else 4

    def build_level(n):
        operator, level, axis, mask = plan[n]
        base = (operator * level_count + level) * 4
        if axis is None:
            def step(j, carry):
                build(slots[n] + j, base + j)
                return carry
            lax.fori_loop(0, 4, step, 0)
        else:
            bit = own_bit(axis, mask)

            def step(j, carry):
                child = bit + j - 2 * bit * j
                build(slots[n] + j, base + 2 * bit + child)
                return carry
            lax.fori_loop(0, 2, step, 0)

    def dot(left, slot):
        return jnp.dot(left, weight[slot], preferred_element_type=jnp.float32)

    def modulate(value, cos_part, sin_part):
        half = value.shape[0] // 2
        shape = (half // tile, tile, coef_count)
        real = value[:half].reshape(shape)
        imag = value[half:].reshape(shape)
        new_real = cos_part * real - sin_part * imag
        new_imag = cos_part * imag + sin_part * real
        return jnp.concatenate(
            [new_real.reshape(half, coef_count), new_imag.reshape(half, coef_count)], axis=0
        ).astype(jnp.bfloat16)

    def gather_rows(ref, c):
        for p in range(2):
            for i in range(sizes[c]):
                for u in range(first):
                    at = (p * sizes[c] + i) * tile + u * second
                    rows[pl.ds(at, second), :] = ref[p, starts[c] + i, u].astype(jnp.float32)
        return rows[: 2 * sizes[c] * tile, :]

    build_level(0)
    own_copy.wait()

    for c in range(chunks):
        moved = modulate(gather_rows(own, c), phase[0, 0], phase[0, 1])
        total[0, chunk(c), :] = dot(moved, slots[0])

    axis, mask = plan[0][2:]
    shift = (partner_of(axis, mask) - lax.axis_index(axis)) * (
        first if axis == "src" else second
    )
    fill_phase(
        len(plan),
        plan[0][0],
        plan[0][1],
        u_own + (shift if axis == "src" else 0),
        v_own + (shift if axis == "tgt" else 0),
    )
    ends = [0] + swaps[1:] + [len(plan) - 1]

    def prepare(s):
        for n in range(ends[s] + 1, ends[s + 1] + 1):
            fill_phase(n, plan[n][0], plan[n][1], u_own, v_own)
            build_level(n)

    prepare(0)
    near[2].wait()
    for p in range(2):
        for u in range(first):
            mirror[p, pl.ds(u * second, second), :] = reflection[p, u]

    def stage(s, c):
        n = swaps[s]
        if s == 0:
            raw_copy(c).wait_recv()
            value = gather_rows(landed, c)
            received = modulate(value, phase[len(plan), 0], phase[len(plan), 1])
        else:
            state_copy(s, c).wait_recv()
            received = held[s - 1, chunk(c), :]
        chunk_rows = 2 * tile * sizes[c]
        row_index = lax.broadcasted_iota(jnp.int32, (chunk_rows, coef_count), 0)
        summed = total[s, chunk(c), :] + dot(received, slots[n] + 1)
        state = summed.astype(jnp.bfloat16).astype(jnp.float32)
        last = swaps[s + 1] if s + 1 < len(swaps) else len(plan)
        for m in range(n + 1, last + 1):
            before = plan[m - 1][0]
            if before == 0 and (m == len(plan) or plan[m][0] == 1):
                state = (
                    modulate(state, mirror[0], mirror[1]).astype(jnp.float32)
                )
            if m == len(plan):
                break
            moved = modulate(state, phase[m, 0], phase[m, 1])
            if m == last:
                sent[s, chunk(c), :] = moved
                state_copy(s + 1, c).start()
                if s == 0 and c + lead < chunks:
                    raw_copy(c + lead).start()
                total[s + 1, chunk(c), :] = dot(moved, slots[m])
                return
            span = plan[m][3]
            upper_row = lax.rem(lax.div(row_index, span), 2) == 1
            wide = moved.astype(jnp.float32)
            lower = jnp.where(upper_row, pltpu.roll(wide, span, 0), wide).astype(jnp.bfloat16)
            upper = jnp.where(
                upper_row, wide, pltpu.roll(wide, chunk_rows - span, 0)
            ).astype(jnp.bfloat16)
            low = dot(lower, slots[m]) + dot(upper, slots[m] + 1)
            high = dot(lower, slots[m] + 2) + dot(upper, slots[m] + 3)
            state = jnp.where(upper_row, high, low).astype(jnp.bfloat16).astype(jnp.float32)
        result = state.astype(jnp.bfloat16).reshape(2, sizes[c], tile, coef_count)
        out[:, pl.ds(starts[c], sizes[c])] = result

    for t in range(chunks + LAG * (len(swaps) - 1)):
        for s in range(len(swaps)):
            if 0 <= t - LAG * s < chunks:
                stage(s, t - LAG * s)
        if 1 <= t + 1 < len(swaps):
            prepare(t + 1)

    for c in range(chunks):
        raw_copy(c).wait_send()
        for s in range(1, len(swaps)):
            state_copy(s, c).wait_send()


def by_swaps(coeffs, reflection, interp, orders):
    level_count = interp.shape[1]
    order_count = interp.shape[-1]
    _, ills, first, second, coef_count = coeffs.shape
    sizes_of = [ills * share // sum(SHARES) for share in SHARES]
    sizes_of[0] += ills - sum(sizes_of)
    sizes_of = [size for size in sizes_of if size > 0]
    chunks = len(sizes_of)
    tile = first * second
    sizes = (lax.axis_size("src"), lax.axis_size("tgt"))
    plan = level_plan(level_count, (first, second), sizes)
    swap_count = sum(item[2] is not None for item in plan)
    slot_count = 2 * swap_count + 4 * (len(plan) - swap_count)
    state_rows = 2 * ills * tile
    later = max(swap_count - 1, 1)
    whole = pl.BlockSpec(memory_space=pltpu.VMEM)
    result = pl.pallas_call(
        functools.partial(swap_kernel, plan, (first, second), sizes_of),
        out_shape=jax.ShapeDtypeStruct((2, ills, tile, coef_count), jnp.bfloat16),
        in_specs=[pl.BlockSpec(memory_space=pl.ANY)] * 4,
        out_specs=whole,
        scratch_shapes=[
            pltpu.VMEM(coeffs.shape, jnp.bfloat16),
            pltpu.VMEM(reflection.shape, jnp.float32),
            pltpu.VMEM(interp.shape, jnp.float32),
            pltpu.VMEM((1, coef_count), jnp.int32),
            pltpu.VMEM(coeffs.shape, jnp.bfloat16),
            pltpu.VMEM((later, state_rows, coef_count), jnp.bfloat16),
            pltpu.VMEM((later, state_rows, coef_count), jnp.bfloat16),
            pltpu.VMEM((swap_count, state_rows, coef_count), jnp.float32),
            pltpu.VMEM((2 * tile * max(sizes_of), coef_count), jnp.float32),
            pltpu.VMEM((3, 8 * level_count * order_count, coef_count), jnp.float32),
            pltpu.VMEM((len(plan) + 1, 2, tile, coef_count), jnp.float32),
            pltpu.VMEM((slot_count, coef_count, coef_count), jnp.bfloat16),
            pltpu.VMEM((2, tile, coef_count), jnp.float32),
            pltpu.SemaphoreType.DMA((4,)),
            pltpu.SemaphoreType.DMA((swap_count, chunks)),
            pltpu.SemaphoreType.DMA((swap_count, chunks)),
        ],
        compiler_params=pltpu.CompilerParams(
            collective_id=0, has_side_effects=True, vmem_limit_bytes=60 * 2**20
        ),
        name="butterfly",
    )(coeffs, reflection, interp, orders.reshape(1, coef_count))
    return result.reshape(coeffs.shape)


def flipped(axis, mask):
    index = lax.axis_index(axis)
    for bit in range(mask.bit_length()):
        if mask >> bit & 1:
            index = index + 2**bit * (1 - 2 * lax.rem(lax.div(index, 2**bit), 2))
    return index


def spread_kernel(
    spans,
    coeffs,
    reflection_far,
    interp_far,
    orders_far,
    out,
    reflection,
    interp,
    orders,
    landed,
    back,
    mirror_out,
    mirror_in,
    rows,
    spread,
    phase,
    mirror,
    weight,
    near_sem,
    send_sem,
    recv_sem,
    back_send_sem,
    back_recv_sem,
    gather_send_sem,
    gather_recv_sem,
    share_send_sem,
    share_recv_sem,
):
    src_span, tgt_span = spans
    chunks = landed.shape[0]
    order_count = interp.shape[-1]
    level_count = interp.shape[1]
    coef_count = coeffs.shape[-1]
    first, second = coeffs.shape[2:4]
    u_count, v_count = src_span * first, tgt_span * second
    box_count = u_count * v_count
    square = order_count * order_count

    u_home = lax.axis_index("src")
    v_home = lax.axis_index("tgt")
    core = lax.axis_index("ill")
    home = u_home * tgt_span + v_home
    offsets = [(du, dv) for du in reversed(range(src_span)) for dv in reversed(range(tgt_span))]

    def device(k):
        return {
            "src": flipped("src", offsets[k][0]),
            "tgt": flipped("tgt", offsets[k][1]),
            "ill": 1 - core,
        }

    def place(k):
        return flipped("src", offsets[k][0]) * tgt_span + flipped("tgt", offsets[k][1])

    beside = [{"tgt": flipped("tgt", dv)} for dv in range(1, tgt_span)]
    partners = [device(k) for k in range(len(offsets))] + beside

    barrier = pltpu.get_barrier_semaphore()
    for partner in partners:
        pl.semaphore_signal(barrier, inc=1, device_id=partner, device_id_type=MESH)

    near = [
        pltpu.make_async_copy(orders_far, orders, near_sem.at[0]),
        pltpu.make_async_copy(reflection_far, reflection, near_sem.at[1]),
        pltpu.make_async_copy(interp_far, interp, near_sem.at[2]),
    ]
    for copy in near:
        copy.start()

    def out_copy(c, k):
        return pltpu.make_async_remote_copy(
            src_ref=coeffs.at[:, pl.ds(place(k) * chunks + c, 1)],
            dst_ref=landed.at[c, home],
            send_sem=send_sem.at[c, k],
            recv_sem=recv_sem.at[c, k],
            device_id=device(k),
            device_id_type=MESH,
        )

    def back_copy(c, k):
        return pltpu.make_async_remote_copy(
            src_ref=back.at[c, place(k)],
            dst_ref=out.at[:, pl.ds(home * chunks + c, 1)],
            send_sem=back_send_sem.at[c, k],
            recv_sem=back_recv_sem.at[c, k],
            device_id=device(k),
            device_id_type=MESH,
        )

    across = [device(k) for k, offset in enumerate(offsets) if not offset[0]] + beside

    def gather_copy(du):
        return pltpu.make_async_remote_copy(
            src_ref=mirror_out.at[core],
            dst_ref=mirror_in.at[core, v_home, u_home],
            send_sem=gather_send_sem.at[du],
            recv_sem=gather_recv_sem.at[du],
            device_id=device(offsets.index((du, 0))),
            device_id_type=MESH,
        )

    def share_copy(du, k):
        block = mirror_in.at[1 - core, v_home, flipped("src", du)]
        return pltpu.make_async_remote_copy(
            src_ref=block,
            dst_ref=block,
            send_sem=share_send_sem.at[du, k],
            recv_sem=share_recv_sem.at[du, k],
            device_id=across[k],
            device_id_type=MESH,
        )

    def share(du):
        if du:
            gather_copy(du).wait_recv()
        for k in range(len(across)):
            share_copy(du, k).start()

    near[1].wait()
    mirror_out[...] = reflection[...].astype(jnp.bfloat16)
    mirror_in[1 - core, v_home, u_home] = mirror_out[1 - core]

    pl.semaphore_wait(barrier, len(partners))
    for du in reversed(range(1, src_span)):
        gather_copy(du).start()
    for k in range(len(offsets)):
        out_copy(0, k).start()
    share(0)
    for c in range(1, chunks):
        for k in range(3 * len(offsets) // 8):
            out_copy(c, k).start()

    near[0].wait()
    digits = (
        lax.div(orders[...], square),
        lax.rem(lax.div(orders[...], order_count), order_count),
        lax.rem(orders[...], order_count),
    )
    values = [
        jnp.cos(math.pi * (2.0 * d.astype(jnp.float32) + 1.0) / (2.0 * order_count))
        for d in digits
    ]

    def times(left, right):
        return (
            left[0] * right[0] - left[1] * right[1],
            left[0] * right[1] + left[1] * right[0],
        )

    def fill_phases(operator):
        direction = DIRECTIONS[operator]
        node = direction[0] * values[0] + direction[1] * values[1]
        node = node + direction[2] * values[2]
        turns = []
        for count, rate in ((u_count, PHASE_RATE), (v_count, PHASE_RATE * ALONG_SECOND)):
            position = lax.broadcasted_iota(jnp.int32, (count, coef_count), 0)
            angle = rate * (position.astype(jnp.float32) + 0.5) * node
            turns.append((jnp.cos(angle), jnp.sin(angle)))
        u_turn, v_turn = turns
        u_now, v_now = u_turn, v_turn
        for level in range(level_count):
            if level:
                u_now, v_now = times(u_now, u_turn), times(v_now, v_turn)
            n = operator * level_count + level
            outer, inner = (u_now, v_now) if n <= level_count else (v_now, u_now)
            span = inner[0].shape[0]
            for i in range(outer[0].shape[0]):
                turn = times((outer[0][i : i + 1], outer[1][i : i + 1]), inner)
                phase[n, 0, pl.ds(i * span, span), :] = turn[0]
                phase[n, 1, pl.ds(i * span, span), :] = turn[1]

    for operator in range(2):
        fill_phases(operator)

    column = lax.broadcasted_iota(jnp.int32, (order_count, coef_count), 1)
    point = lax.broadcasted_iota(jnp.int32, (order_count, coef_count), 0)
    column_digits = (
        lax.div(column, square),
        lax.rem(lax.div(column, order_count), order_count),
        lax.rem(column, order_count),
    )
    near[2].wait()
    for d in range(3):
        selector = (point == column_digits[d]).astype(jnp.float32)
        factors = interp[:, :, :, :, d].reshape(-1, order_count, order_count)
        factors = jnp.swapaxes(factors, 1, 2).reshape(-1, order_count)
        spread[d] = jnp.dot(
            factors, selector, precision=lax.Precision.HIGHEST,
            preferred_element_type=jnp.float32,
        )

    def build(index, carry):
        where = pl.ds(pl.multiple_of(index * order_count, order_count), order_count)
        n = lax.div(index, 4)
        side = lax.rem(lax.div(index, 2), 2)
        child = lax.rem(index, 2)
        columns = pl.ds(pl.multiple_of(side * coef_count, coef_count), coef_count)
        first_factor = spread[0, where, :]
        second_factor = spread[1, where, :]
        third_factor = spread[2, where, :]
        for a in range(order_count):
            pair = first_factor[a : a + 1, :] * second_factor
            block = pair[:, None, :] * third_factor[None, :, :]
            at = pl.multiple_of(child * coef_count + a * square, square)
            weight[n, pl.ds(at, square), columns] = block.reshape(square, coef_count).astype(
                jnp.bfloat16
            )
        return carry

    marks = (0, 4 * level_count, 4 * level_count, 8 * level_count)
    lax.fori_loop(marks[0], marks[1], build, 0)
    for du in range(1, src_span - 1):
        share(du)
    lax.fori_loop(marks[1], marks[2], build, 0)
    if src_span > 1:
        share(src_span - 1)
    for c in range(1, chunks):
        for k in range(3 * len(offsets) // 8, len(offsets)):
            out_copy(c, k).start()
    lax.fori_loop(marks[2], marks[3], build, 0)

    def modulate(blocks, table, n):
        result = [[], []]
        for i, (real, imag) in enumerate(zip(*blocks)):
            span = real.shape[0]
            at = pl.ds(i * span, span)
            new = times((table[n, 0, at, :], table[n, 1, at, :]), (real, imag))
            result[0].append(new[0])
            result[1].append(new[1])
        return result

    def apply_level(blocks, n, bit):
        count = len(blocks[0])
        low = [i for i in range(count) if not i >> bit & 1]
        parts = [
            jnp.concatenate([blocks[p][i + side * 2**bit] for p in range(2) for i in low], axis=0)
            for side in range(2)
        ]
        left = jnp.concatenate(parts, axis=1).astype(jnp.bfloat16)
        left = jnp.concatenate([left] * max(1, FULL_ROWS // left.shape[0]), axis=0)
        result = jnp.dot(left, weight[n], preferred_element_type=jnp.float32)
        new = [[None] * count, [None] * count]
        span = blocks[0][0].shape[0]
        for p in range(2):
            for at, i in enumerate(low):
                start = (p * len(low) + at) * span
                for side in range(2):
                    new[p][i + side * 2**bit] = result[
                        start : start + span, side * coef_count : (side + 1) * coef_count
                    ]
        return new

    def place_blocks(blocks):
        for p in range(2):
            for i, block in enumerate(blocks[p]):
                span = block.shape[0]
                lanes = rows.shape[-1]
                for g in range(rows.shape[0]):
                    rows[g, pl.ds(p * box_count + i * span, span), :] = block[
                        :, g * lanes : (g + 1) * lanes
                    ]

    def take(start, count, stride):
        return jnp.concatenate(
            [rows[g, pl.ds(start, count, stride), :] for g in range(rows.shape[0])], axis=1
        )

    def run(c):
        for k in range(len(offsets)):
            out_copy(c, k).wait_recv()
        lanes = rows.shape[-1]
        for p in range(2):
            for s in range(src_span):
                for t in range(tgt_span):
                    for i in range(first):
                        at = p * box_count + (s * first + i) * v_count + t * second
                        piece = landed[c, s * tgt_span + t, p, 0, i].astype(jnp.float32)
                        for g in range(rows.shape[0]):
                            rows[g, pl.ds(at, second), :] = piece[:, g * lanes : (g + 1) * lanes]
        blocks = [
            [take(p * box_count + i * v_count, v_count, 1) for i in range(u_count)]
            for p in range(2)
        ]
        u_top = u_count.bit_length() - 2
        v_top = v_count.bit_length() - 2
        for level in range(level_count):
            blocks = apply_level(modulate(blocks, phase, level), level, u_top - level)
        if c == 0:
            for du in range(src_span):
                for k in range(len(across)):
                    share_copy(du, k).wait_recv()
            for p in range(2):
                for s in range(src_span):
                    for t in range(tgt_span):
                        for i in range(first):
                            at = (s * first + i) * v_count + t * second
                            mirror[0, p, pl.ds(at, second), :] = mirror_in[
                                p, t, s, i
                            ].astype(jnp.float32)
            for i in range(u_count):
                at = pl.ds(i * v_count, v_count)
                both = times(
                    (mirror[0, 0, at, :], mirror[0, 1, at, :]),
                    (phase[level_count, 0, at, :], phase[level_count, 1, at, :]),
                )
                mirror[0, 0, at, :] = both[0]
                mirror[0, 1, at, :] = both[1]
        place_blocks(modulate(blocks, mirror, 0))
        blocks = [
            [take(p * box_count + i, u_count, v_count) for i in range(v_count)] for p in range(2)
        ]
        for level in range(level_count):
            n = level_count + level
            if level:
                blocks = modulate(blocks, phase, n)
            blocks = apply_level(blocks, n, v_top - level)
        place_blocks(blocks)
        for s in range(src_span):
            for t in range(tgt_span):
                for p in range(2):
                    for i in range(first):
                        at = p * box_count + t * second * u_count + s * first + i
                        back[c, s * tgt_span + t, p, 0, i] = take(at, second, u_count).astype(
                            jnp.bfloat16
                        )
        for k in range(len(offsets)):
            back_copy(c, k).start()

    for c in range(chunks):
        run(c)
    for du in range(src_span):
        if du:
            gather_copy(du).wait_send()
        for k in range(len(across)):
            share_copy(du, k).wait_send()
    for c in range(chunks):
        for k in range(len(offsets)):
            out_copy(c, k).wait_send()
    for c in range(chunks):
        for k in range(len(offsets)):
            back_copy(c, k).wait_send()
        for k in reversed(range(len(offsets))):
            back_copy(c, k).wait_recv()


def by_spreading(coeffs, reflection, interp, orders):
    level_count = interp.shape[1]
    order_count = interp.shape[-1]
    _, ills, first, second, coef_count = coeffs.shape
    spans = (lax.axis_size("src"), lax.axis_size("tgt"))
    places = spans[0] * spans[1]
    chunks = ills // places
    box_count = places * first * second
    lanes = min(128, coef_count)
    far = pl.BlockSpec(memory_space=pltpu.HBM)
    operands = [
        pltpu.with_memory_space_constraint(operand, pltpu.HBM)
        for operand in (coeffs, reflection, interp, orders.reshape(1, coef_count))
    ]
    return pl.pallas_call(
        functools.partial(spread_kernel, spans),
        out_shape=jax.ShapeDtypeStruct(coeffs.shape, jnp.bfloat16),
        in_specs=[far] * 4,
        out_specs=pl.BlockSpec(memory_space=pltpu.VMEM),
        scratch_shapes=[
            pltpu.VMEM(reflection.shape, jnp.float32),
            pltpu.VMEM(interp.shape, jnp.float32),
            pltpu.VMEM((1, coef_count), jnp.int32),
            pltpu.VMEM((chunks, places, 2, 1, first, second, coef_count), jnp.bfloat16),
            pltpu.VMEM((chunks, places, 2, 1, first, second, coef_count), jnp.bfloat16),
            pltpu.VMEM(reflection.shape, jnp.bfloat16),
            pltpu.VMEM((2, spans[1], spans[0], first, second, coef_count), jnp.bfloat16),
            pltpu.VMEM((coef_count // lanes, 2 * box_count, lanes), jnp.float32),
            pltpu.VMEM((3, 8 * level_count * order_count, coef_count), jnp.float32),
            pltpu.VMEM((2 * level_count, 2, box_count, coef_count), jnp.float32),
            pltpu.VMEM((1, 2, box_count, coef_count), jnp.float32),
            pltpu.VMEM((2 * level_count, 2 * coef_count, 2 * coef_count), jnp.bfloat16),
            pltpu.SemaphoreType.DMA((3,)),
            pltpu.SemaphoreType.DMA((chunks, places)),
            pltpu.SemaphoreType.DMA((chunks, places)),
            pltpu.SemaphoreType.DMA((chunks, places)),
            pltpu.SemaphoreType.DMA((chunks, places)),
            pltpu.SemaphoreType.DMA((spans[0],)),
            pltpu.SemaphoreType.DMA((spans[0],)),
            pltpu.SemaphoreType.DMA((spans[0], 2 * spans[1])),
            pltpu.SemaphoreType.DMA((spans[0], 2 * spans[1])),
        ],
        compiler_params=pltpu.CompilerParams(
            collective_id=0, has_side_effects=True, vmem_limit_bytes=40 * 2**20
        ),
        name="butterfly",
    )(*operands)


def on_device(coeffs, reflection, interp, orders):
    level_count = interp.shape[1]
    _, ills, first, second, _ = coeffs.shape
    spans = (lax.axis_size("src"), lax.axis_size("tgt"))
    covers = spans[0] * first == 2**level_count and spans[1] * second == 2**level_count
    if covers and ills % (spans[0] * spans[1]) == 0 and lax.axis_size("ill") == 2:
        return by_spreading(coeffs, reflection, interp, orders)
    return by_swaps(coeffs, reflection, interp, orders)


def solution(mesh):
    in_specs = (
        P(None, ("groups", "ill"), "src", "tgt", None),
        P(None, ("groups", "src"), "tgt", None),
        P(),
        P(),
    )
    out_specs = P(None, ("groups", "ill"), "src", "tgt", None)
    return jax.shard_map(
        on_device, mesh=mesh, in_specs=in_specs, out_specs=out_specs, check_vma=False
    )
```

```python
import functools
import math

import jax
import jax.numpy as jnp
from jax import lax
from jax.experimental import pallas as pl
from jax.experimental.pallas import tpu as pltpu
from jax.sharding import PartitionSpec as P

PHASE_RATE = 0.3
ALONG_SECOND = 1.7
DIRECTIONS = ((0.6, 0.48, 0.64), (-0.36, 0.8, 0.48))
SHARES = (2, 4, 5, 5)
LEAD = 3
LAG = 2
FULL_ROWS = 128
MESH = pl.DeviceIdType.MESH


def level_plan(level_count, boxes, sizes):
    plan = []
    for operator, axis in enumerate(("src", "tgt")):
        local_bits = boxes[operator].bit_length() - 1
        top_bit = (boxes[operator] * sizes[operator]).bit_length() - 2
        row_span = boxes[1] if operator == 0 else 1
        for level in range(level_count):
            bit = top_bit - level
            if bit >= local_bits:
                plan.append((operator, level, axis, 2 ** (bit - local_bits)))
            else:
                plan.append((operator, level, None, row_span * 2**bit))
    return plan


def own_bit(axis, mask):
    return lax.rem(lax.div(lax.axis_index(axis), mask), 2)


def partner_of(axis, mask):
    return lax.axis_index(axis) + mask * (1 - 2 * own_bit(axis, mask))


def swap_kernel(
    plan,
    boxes,
    sizes,
    coeffs,
    reflection_far,
    interp_far,
    orders_far,
    out,
    own,
    reflection,
    interp,
    orders,
    landed,
    held,
    sent,
    total,
    rows,
    spread,
    phase,
    weight,
    mirror,
    own_sem,
    send_sem,
    recv_sem,
):
    order_count = interp.shape[-1]
    coef_count = coeffs.shape[-1]
    first, second = boxes
    tile = first * second
    chunks = len(sizes)
    starts = [sum(sizes[:c]) for c in range(chunks)]
    swaps = [n for n, item in enumerate(plan) if item[2] is not None]

    def chunk(c):
        return pl.ds(2 * tile * starts[c], 2 * tile * sizes[c])

    barrier = pltpu.get_barrier_semaphore()
    for n in swaps:
        axis, mask = plan[n][2:]
        pl.semaphore_signal(
            barrier, inc=1, device_id={axis: partner_of(axis, mask)}, device_id_type=MESH
        )
    pl.semaphore_wait(barrier, len(swaps))

    def raw_copy(c):
        axis, mask = plan[0][2:]
        return pltpu.make_async_remote_copy(
            src_ref=coeffs.at[:, pl.ds(starts[c], sizes[c])],
            dst_ref=landed.at[:, pl.ds(starts[c], sizes[c])],
            send_sem=send_sem.at[0, c],
            recv_sem=recv_sem.at[0, c],
            device_id={axis: partner_of(axis, mask)},
            device_id_type=MESH,
        )

    def state_copy(s, c):
        axis, mask = plan[swaps[s]][2:]
        return pltpu.make_async_remote_copy(
            src_ref=sent.at[s - 1, chunk(c)],
            dst_ref=held.at[s - 1, chunk(c)],
            send_sem=send_sem.at[s, c],
            recv_sem=recv_sem.at[s, c],
            device_id={axis: partner_of(axis, mask)},
            device_id_type=MESH,
        )

    lead = min(LEAD, chunks) if len(swaps) > 1 else chunks
    for c in range(lead):
        raw_copy(c).start()
    own_copy = pltpu.make_async_copy(coeffs, own, own_sem.at[0])
    near = [
        pltpu.make_async_copy(orders_far, orders, own_sem.at[1]),
        pltpu.make_async_copy(interp_far, interp, own_sem.at[2]),
        pltpu.make_async_copy(reflection_far, reflection, own_sem.at[3]),
    ]
    for copy in near:
        copy.start()
    own_copy.start()
    near[0].wait()

    digits = (
        lax.div(orders[...], order_count * order_count),
        lax.rem(lax.div(orders[...], order_count), order_count),
        lax.rem(orders[...], order_count),
    )
    values = [
        jnp.cos(math.pi * (2.0 * d.astype(jnp.float32) + 1.0) / (2.0 * order_count))
        for d in digits
    ]
    products = []
    for direction in DIRECTIONS:
        summed = direction[0] * values[0] + direction[1] * values[1]
        products.append(summed + direction[2] * values[2])
    row = lax.broadcasted_iota(jnp.int32, (tile, coef_count), 0)

    def fill_phase(slot, operator, level, u_start, v_start):
        u = (lax.div(row, second) + u_start).astype(jnp.float32)
        v = (lax.rem(row, second) + v_start).astype(jnp.float32)
        position = (u + 0.5) + ALONG_SECOND * (v + 0.5)
        angle = (PHASE_RATE * (level + 1)) * position * products[operator]
        phase[slot, 0] = jnp.cos(angle).astype(jnp.bfloat16).astype(jnp.float32)
        phase[slot, 1] = jnp.sin(angle).astype(jnp.bfloat16).astype(jnp.float32)

    u_own = lax.axis_index("src") * first
    v_own = lax.axis_index("tgt") * second
    fill_phase(0, plan[0][0], plan[0][1], u_own, v_own)

    column = lax.broadcasted_iota(jnp.int32, (order_count, coef_count), 1)
    point = lax.broadcasted_iota(jnp.int32, (order_count, coef_count), 0)
    column_digits = (
        lax.div(column, order_count * order_count),
        lax.rem(lax.div(column, order_count), order_count),
        lax.rem(column, order_count),
    )
    near[1].wait()
    for d in range(3):
        selector = (point == column_digits[d]).astype(jnp.float32)
        factors = interp[:, :, :, :, d].reshape(-1, order_count, order_count)
        factors = jnp.swapaxes(factors, 1, 2).reshape(-1, order_count)
        spread[d] = jnp.dot(
            factors, selector, precision=lax.Precision.HIGHEST,
            preferred_element_type=jnp.float32,
        )

    square = order_count * order_count

    def build(slot, index):
        where = pl.ds(pl.multiple_of(index * order_count, order_count), order_count)
        first_factor = spread[0, where, :]
        second_factor = spread[1, where, :]
        third_factor = spread[2, where, :]
        for a in range(order_count):
            pair = first_factor[a : a + 1, :] * second_factor
            block = pair[:, None, :] * third_factor[None, :, :]
            weight[slot, pl.ds(a * square, square), :] = block.reshape(
                square, coef_count
            ).astype(jnp.bfloat16)

    level_count = interp.shape[1]
    slots = []
    used = 0
    for item in plan:
        slots.append(used)
        used += 2 if item[2] is not None else 4

    def build_level(n):
        operator, level, axis, mask = plan[n]
        base = (operator * level_count + level) * 4
        if axis is None:
            def step(j, carry):
                build(slots[n] + j, base + j)
                return carry
            lax.fori_loop(0, 4, step, 0)
        else:
            bit = own_bit(axis, mask)

            def step(j, carry):
                child = bit + j - 2 * bit * j
                build(slots[n] + j, base + 2 * bit + child)
                return carry
            lax.fori_loop(0, 2, step, 0)

    def dot(left, slot):
        return jnp.dot(left, weight[slot], preferred_element_type=jnp.float32)

    def modulate(value, cos_part, sin_part):
        half = value.shape[0] // 2
        shape = (half // tile, tile, coef_count)
        real = value[:half].reshape(shape)
        imag = value[half:].reshape(shape)
        new_real = cos_part * real - sin_part * imag
        new_imag = cos_part * imag + sin_part * real
        return jnp.concatenate(
            [new_real.reshape(half, coef_count), new_imag.reshape(half, coef_count)], axis=0
        ).astype(jnp.bfloat16)

    def gather_rows(ref, c):
        for p in range(2):
            for i in range(sizes[c]):
                for u in range(first):
                    at = (p * sizes[c] + i) * tile + u * second
                    rows[pl.ds(at, second), :] = ref[p, starts[c] + i, u].astype(jnp.float32)
        return rows[: 2 * sizes[c] * tile, :]

    build_level(0)
    own_copy.wait()

    for c in range(chunks):
        moved = modulate(gather_rows(own, c), phase[0, 0], phase[0, 1])
        total[0, chunk(c), :] = dot(moved, slots[0])

    axis, mask = plan[0][2:]
    shift = (partner_of(axis, mask) - lax.axis_index(axis)) * (
        first if axis == "src" else second
    )
    fill_phase(
        len(plan),
        plan[0][0],
        plan[0][1],
        u_own + (shift if axis == "src" else 0),
        v_own + (shift if axis == "tgt" else 0),
    )
    ends = [0] + swaps[1:] + [len(plan) - 1]

    def prepare(s):
        for n in range(ends[s] + 1, ends[s + 1] + 1):
            fill_phase(n, plan[n][0], plan[n][1], u_own, v_own)
            build_level(n)

    prepare(0)
    near[2].wait()
    for p in range(2):
        for u in range(first):
            mirror[p, pl.ds(u * second, second), :] = reflection[p, u]

    def stage(s, c):
        n = swaps[s]
        if s == 0:
            raw_copy(c).wait_recv()
            value = gather_rows(landed, c)
            received = modulate(value, phase[len(plan), 0], phase[len(plan), 1])
        else:
            state_copy(s, c).wait_recv()
            received = held[s - 1, chunk(c), :]
        chunk_rows = 2 * tile * sizes[c]
        row_index = lax.broadcasted_iota(jnp.int32, (chunk_rows, coef_count), 0)
        summed = total[s, chunk(c), :] + dot(received, slots[n] + 1)
        state = summed.astype(jnp.bfloat16).astype(jnp.float32)
        last = swaps[s + 1] if s + 1 < len(swaps) else len(plan)
        for m in range(n + 1, last + 1):
            before = plan[m - 1][0]
            if before == 0 and (m == len(plan) or plan[m][0] == 1):
                state = (
                    modulate(state, mirror[0], mirror[1]).astype(jnp.float32)
                )
            if m == len(plan):
                break
            moved = modulate(state, phase[m, 0], phase[m, 1])
            if m == last:
                sent[s, chunk(c), :] = moved
                state_copy(s + 1, c).start()
                if s == 0 and c + lead < chunks:
                    raw_copy(c + lead).start()
                total[s + 1, chunk(c), :] = dot(moved, slots[m])
                return
            span = plan[m][3]
            upper_row = lax.rem(lax.div(row_index, span), 2) == 1
            wide = moved.astype(jnp.float32)
            lower = jnp.where(upper_row, pltpu.roll(wide, span, 0), wide).astype(jnp.bfloat16)
            upper = jnp.where(
                upper_row, wide, pltpu.roll(wide, chunk_rows - span, 0)
            ).astype(jnp.bfloat16)
            low = dot(lower, slots[m]) + dot(upper, slots[m] + 1)
            high = dot(lower, slots[m] + 2) + dot(upper, slots[m] + 3)
            state = jnp.where(upper_row, high, low).astype(jnp.bfloat16).astype(jnp.float32)
        result = state.astype(jnp.bfloat16).reshape(2, sizes[c], tile, coef_count)
        out[:, pl.ds(starts[c], sizes[c])] = result

    for t in range(chunks + LAG * (len(swaps) - 1)):
        for s in range(len(swaps)):
            if 0 <= t - LAG * s < chunks:
                stage(s, t - LAG * s)
        if 1 <= t + 1 < len(swaps):
            prepare(t + 1)

    for c in range(chunks):
        raw_copy(c).wait_send()
        for s in range(1, len(swaps)):
            state_copy(s, c).wait_send()


def by_swaps(coeffs, reflection, interp, orders):
    level_count = interp.shape[1]
    order_count = interp.shape[-1]
    _, ills, first, second, coef_count = coeffs.shape
    sizes_of = [ills * share // sum(SHARES) for share in SHARES]
    sizes_of[0] += ills - sum(sizes_of)
    sizes_of = [size for size in sizes_of if size > 0]
    chunks = len(sizes_of)
    tile = first * second
    sizes = (lax.axis_size("src"), lax.axis_size("tgt"))
    plan = level_plan(level_count, (first, second), sizes)
    swap_count = sum(item[2] is not None for item in plan)
    slot_count = 2 * swap_count + 4 * (len(plan) - swap_count)
    state_rows = 2 * ills * tile
    later = max(swap_count - 1, 1)
    whole = pl.BlockSpec(memory_space=pltpu.VMEM)
    result = pl.pallas_call(
        functools.partial(swap_kernel, plan, (first, second), sizes_of),
        out_shape=jax.ShapeDtypeStruct((2, ills, tile, coef_count), jnp.bfloat16),
        in_specs=[pl.BlockSpec(memory_space=pl.ANY)] * 4,
        out_specs=whole,
        scratch_shapes=[
            pltpu.VMEM(coeffs.shape, jnp.bfloat16),
            pltpu.VMEM(reflection.shape, jnp.float32),
            pltpu.VMEM(interp.shape, jnp.float32),
            pltpu.VMEM((1, coef_count), jnp.int32),
            pltpu.VMEM(coeffs.shape, jnp.bfloat16),
            pltpu.VMEM((later, state_rows, coef_count), jnp.bfloat16),
            pltpu.VMEM((later, state_rows, coef_count), jnp.bfloat16),
            pltpu.VMEM((swap_count, state_rows, coef_count), jnp.float32),
            pltpu.VMEM((2 * tile * max(sizes_of), coef_count), jnp.float32),
            pltpu.VMEM((3, 8 * level_count * order_count, coef_count), jnp.float32),
            pltpu.VMEM((len(plan) + 1, 2, tile, coef_count), jnp.float32),
            pltpu.VMEM((slot_count, coef_count, coef_count), jnp.bfloat16),
            pltpu.VMEM((2, tile, coef_count), jnp.float32),
            pltpu.SemaphoreType.DMA((4,)),
            pltpu.SemaphoreType.DMA((swap_count, chunks)),
            pltpu.SemaphoreType.DMA((swap_count, chunks)),
        ],
        compiler_params=pltpu.CompilerParams(
            collective_id=0, has_side_effects=True, vmem_limit_bytes=60 * 2**20
        ),
        name="butterfly",
    )(coeffs, reflection, interp, orders.reshape(1, coef_count))
    return result.reshape(coeffs.shape)


def flipped(axis, mask):
    index = lax.axis_index(axis)
    for bit in range(mask.bit_length()):
        if mask >> bit & 1:
            index = index + 2**bit * (1 - 2 * lax.rem(lax.div(index, 2**bit), 2))
    return index


def spread_kernel(
    spans,
    coeffs,
    reflection_far,
    interp_far,
    orders_far,
    out,
    reflection,
    interp,
    orders,
    landed,
    back,
    mirror_out,
    mirror_in,
    rows,
    spread,
    phase,
    mirror,
    weight,
    near_sem,
    send_sem,
    recv_sem,
    back_send_sem,
    back_recv_sem,
    gather_send_sem,
    gather_recv_sem,
    share_send_sem,
    share_recv_sem,
):
    src_span, tgt_span = spans
    chunks = landed.shape[0]
    order_count = interp.shape[-1]
    level_count = interp.shape[1]
    coef_count = coeffs.shape[-1]
    first, second = coeffs.shape[2:4]
    u_count, v_count = src_span * first, tgt_span * second
    box_count = u_count * v_count
    square = order_count * order_count

    u_home = lax.axis_index("src")
    v_home = lax.axis_index("tgt")
    core = lax.axis_index("ill")
    home = u_home * tgt_span + v_home
    offsets = [(du, dv) for du in reversed(range(src_span)) for dv in reversed(range(tgt_span))]

    def device(k):
        return {
            "src": flipped("src", offsets[k][0]),
            "tgt": flipped("tgt", offsets[k][1]),
            "ill": 1 - core,
        }

    def place(k):
        return flipped("src", offsets[k][0]) * tgt_span + flipped("tgt", offsets[k][1])

    beside = [{"tgt": flipped("tgt", dv)} for dv in range(1, tgt_span)]
    partners = [device(k) for k in range(len(offsets))] + beside

    barrier = pltpu.get_barrier_semaphore()
    for partner in partners:
        pl.semaphore_signal(barrier, inc=1, device_id=partner, device_id_type=MESH)

    near = [
        pltpu.make_async_copy(orders_far, orders, near_sem.at[0]),
        pltpu.make_async_copy(reflection_far, reflection, near_sem.at[1]),
        pltpu.make_async_copy(interp_far, interp, near_sem.at[2]),
    ]
    for copy in near:
        copy.start()

    def out_copy(c, k):
        return pltpu.make_async_remote_copy(
            src_ref=coeffs.at[:, pl.ds(place(k) * chunks + c, 1)],
            dst_ref=landed.at[c, home],
            send_sem=send_sem.at[c, k],
            recv_sem=recv_sem.at[c],
            device_id=device(k),
            device_id_type=MESH,
        )

    def back_copy(c, k):
        return pltpu.make_async_remote_copy(
            src_ref=back.at[c, place(k)],
            dst_ref=out.at[:, pl.ds(home * chunks + c, 1)],
            send_sem=back_send_sem.at[c, k],
            recv_sem=back_recv_sem.at[c, k],
            device_id=device(k),
            device_id_type=MESH,
        )

    across = [device(k) for k, offset in enumerate(offsets) if not offset[0]] + beside

    def gather_copy(du):
        return pltpu.make_async_remote_copy(
            src_ref=mirror_out.at[core],
            dst_ref=mirror_in.at[core, v_home, u_home],
            send_sem=gather_send_sem.at[du],
            recv_sem=gather_recv_sem.at[du],
            device_id=device(offsets.index((du, 0))),
            device_id_type=MESH,
        )

    def share_copy(du, k):
        block = mirror_in.at[1 - core, v_home, flipped("src", du)]
        return pltpu.make_async_remote_copy(
            src_ref=block,
            dst_ref=block,
            send_sem=share_send_sem.at[du, k],
            recv_sem=share_recv_sem.at[du, k],
            device_id=across[k],
            device_id_type=MESH,
        )

    def share(du):
        if du:
            gather_copy(du).wait_recv()
        for k in range(len(across)):
            share_copy(du, k).start()

    near[1].wait()
    mirror_out[...] = reflection[...].astype(jnp.bfloat16)
    mirror_in[1 - core, v_home, u_home] = mirror_out[1 - core]

    pl.semaphore_wait(barrier, len(partners))
    for du in reversed(range(1, src_span)):
        gather_copy(du).start()
    for k in range(len(offsets)):
        out_copy(0, k).start()
    share(0)
    for c in range(1, chunks):
        for k in range(3 * len(offsets) // 8):
            out_copy(c, k).start()

    near[0].wait()
    digits = (
        lax.div(orders[...], square),
        lax.rem(lax.div(orders[...], order_count), order_count),
        lax.rem(orders[...], order_count),
    )
    values = [
        jnp.cos(math.pi * (2.0 * d.astype(jnp.float32) + 1.0) / (2.0 * order_count))
        for d in digits
    ]

    def times(left, right):
        return (
            left[0] * right[0] - left[1] * right[1],
            left[0] * right[1] + left[1] * right[0],
        )

    def fill_phases(operator):
        direction = DIRECTIONS[operator]
        node = direction[0] * values[0] + direction[1] * values[1]
        node = node + direction[2] * values[2]
        turns = []
        for count, rate in ((u_count, PHASE_RATE), (v_count, PHASE_RATE * ALONG_SECOND)):
            position = lax.broadcasted_iota(jnp.int32, (count, coef_count), 0)
            angle = rate * (position.astype(jnp.float32) + 0.5) * node
            turns.append((jnp.cos(angle), jnp.sin(angle)))
        u_turn, v_turn = turns
        u_now, v_now = u_turn, v_turn
        for level in range(level_count):
            if level:
                u_now, v_now = times(u_now, u_turn), times(v_now, v_turn)
            n = operator * level_count + level
            outer, inner = (u_now, v_now) if n <= level_count else (v_now, u_now)
            span = inner[0].shape[0]
            for i in range(outer[0].shape[0]):
                turn = times((outer[0][i : i + 1], outer[1][i : i + 1]), inner)
                phase[n, 0, pl.ds(i * span, span), :] = turn[0]
                phase[n, 1, pl.ds(i * span, span), :] = turn[1]

    for operator in range(2):
        fill_phases(operator)

    column = lax.broadcasted_iota(jnp.int32, (order_count, coef_count), 1)
    point = lax.broadcasted_iota(jnp.int32, (order_count, coef_count), 0)
    column_digits = (
        lax.div(column, square),
        lax.rem(lax.div(column, order_count), order_count),
        lax.rem(column, order_count),
    )
    near[2].wait()
    for d in range(3):
        selector = (point == column_digits[d]).astype(jnp.float32)
        factors = interp[:, :, :, :, d].reshape(-1, order_count, order_count)
        factors = jnp.swapaxes(factors, 1, 2).reshape(-1, order_count)
        spread[d] = jnp.dot(
            factors, selector, precision=lax.Precision.HIGHEST,
            preferred_element_type=jnp.float32,
        )

    def build(index, carry):
        where = pl.ds(pl.multiple_of(index * order_count, order_count), order_count)
        n = lax.div(index, 4)
        side = lax.rem(lax.div(index, 2), 2)
        child = lax.rem(index, 2)
        columns = pl.ds(pl.multiple_of(side * coef_count, coef_count), coef_count)
        first_factor = spread[0, where, :]
        second_factor = spread[1, where, :]
        third_factor = spread[2, where, :]
        for a in range(order_count):
            pair = first_factor[a : a + 1, :] * second_factor
            block = pair[:, None, :] * third_factor[None, :, :]
            at = pl.multiple_of(child * coef_count + a * square, square)
            weight[n, pl.ds(at, square), columns] = block.reshape(square, coef_count).astype(
                jnp.bfloat16
            )
        return carry

    marks = (0, 4 * level_count, 4 * level_count, 8 * level_count)
    lax.fori_loop(marks[0], marks[1], build, 0)
    for du in range(1, src_span - 1):
        share(du)
    lax.fori_loop(marks[1], marks[2], build, 0)
    if src_span > 1:
        share(src_span - 1)
    for c in range(1, chunks):
        for k in range(3 * len(offsets) // 8, len(offsets)):
            out_copy(c, k).start()
    lax.fori_loop(marks[2], marks[3], build, 0)

    def modulate(blocks, table, n):
        result = [[], []]
        for i, (real, imag) in enumerate(zip(*blocks)):
            span = real.shape[0]
            at = pl.ds(i * span, span)
            new = times((table[n, 0, at, :], table[n, 1, at, :]), (real, imag))
            result[0].append(new[0])
            result[1].append(new[1])
        return result

    def apply_level(blocks, n, bit):
        count = len(blocks[0])
        low = [i for i in range(count) if not i >> bit & 1]
        parts = [
            jnp.concatenate([blocks[p][i + side * 2**bit] for p in range(2) for i in low], axis=0)
            for side in range(2)
        ]
        left = jnp.concatenate(parts, axis=1).astype(jnp.bfloat16)
        left = jnp.concatenate([left] * max(1, FULL_ROWS // left.shape[0]), axis=0)
        result = jnp.dot(left, weight[n], preferred_element_type=jnp.float32)
        new = [[None] * count, [None] * count]
        span = blocks[0][0].shape[0]
        for p in range(2):
            for at, i in enumerate(low):
                start = (p * len(low) + at) * span
                for side in range(2):
                    new[p][i + side * 2**bit] = result[
                        start : start + span, side * coef_count : (side + 1) * coef_count
                    ]
        return new

    def place_blocks(blocks):
        for p in range(2):
            for i, block in enumerate(blocks[p]):
                span = block.shape[0]
                lanes = rows.shape[-1]
                for g in range(rows.shape[0]):
                    rows[g, pl.ds(p * box_count + i * span, span), :] = block[
                        :, g * lanes : (g + 1) * lanes
                    ]

    def take(start, count, stride):
        return jnp.concatenate(
            [rows[g, pl.ds(start, count, stride), :] for g in range(rows.shape[0])], axis=1
        )

    def run(c):
        pltpu.make_async_copy(landed.at[c], landed.at[c], recv_sem.at[c]).wait()
        lanes = rows.shape[-1]
        for p in range(2):
            for s in range(src_span):
                for t in range(tgt_span):
                    for i in range(first):
                        at = p * box_count + (s * first + i) * v_count + t * second
                        piece = landed[c, s * tgt_span + t, p, 0, i].astype(jnp.float32)
                        for g in range(rows.shape[0]):
                            rows[g, pl.ds(at, second), :] = piece[:, g * lanes : (g + 1) * lanes]
        blocks = [
            [take(p * box_count + i * v_count, v_count, 1) for i in range(u_count)]
            for p in range(2)
        ]
        u_top = u_count.bit_length() - 2
        v_top = v_count.bit_length() - 2
        for level in range(level_count):
            blocks = apply_level(modulate(blocks, phase, level), level, u_top - level)
        if c == 0:
            for du in range(src_span):
                for k in range(len(across)):
                    share_copy(du, k).wait_recv()
            for p in range(2):
                for s in range(src_span):
                    for t in range(tgt_span):
                        for i in range(first):
                            at = (s * first + i) * v_count + t * second
                            mirror[0, p, pl.ds(at, second), :] = mirror_in[
                                p, t, s, i
                            ].astype(jnp.float32)
            for i in range(u_count):
                at = pl.ds(i * v_count, v_count)
                both = times(
                    (mirror[0, 0, at, :], mirror[0, 1, at, :]),
                    (phase[level_count, 0, at, :], phase[level_count, 1, at, :]),
                )
                mirror[0, 0, at, :] = both[0]
                mirror[0, 1, at, :] = both[1]
        place_blocks(modulate(blocks, mirror, 0))
        blocks = [
            [take(p * box_count + i, u_count, v_count) for i in range(v_count)] for p in range(2)
        ]
        for level in range(level_count):
            n = level_count + level
            if level:
                blocks = modulate(blocks, phase, n)
            blocks = apply_level(blocks, n, v_top - level)
        place_blocks(blocks)
        for s in range(src_span):
            for t in range(tgt_span):
                for p in range(2):
                    for i in range(first):
                        at = p * box_count + t * second * u_count + s * first + i
                        back[c, s * tgt_span + t, p, 0, i] = take(at, second, u_count).astype(
                            jnp.bfloat16
                        )
        for k in range(len(offsets)):
            back_copy(c, k).start()

    for c in range(chunks):
        run(c)
    for du in range(src_span):
        if du:
            gather_copy(du).wait_send()
        for k in range(len(across)):
            share_copy(du, k).wait_send()
    for c in range(chunks):
        for k in range(len(offsets)):
            out_copy(c, k).wait_send()
    for c in range(chunks):
        for k in range(len(offsets)):
            back_copy(c, k).wait_send()
        for k in reversed(range(len(offsets))):
            back_copy(c, k).wait_recv()


def by_spreading(coeffs, reflection, interp, orders):
    level_count = interp.shape[1]
    order_count = interp.shape[-1]
    _, ills, first, second, coef_count = coeffs.shape
    spans = (lax.axis_size("src"), lax.axis_size("tgt"))
    places = spans[0] * spans[1]
    chunks = ills // places
    box_count = places * first * second
    lanes = min(128, coef_count)
    far = pl.BlockSpec(memory_space=pltpu.HBM)
    operands = [
        pltpu.with_memory_space_constraint(operand, pltpu.HBM)
        for operand in (coeffs, reflection, interp, orders.reshape(1, coef_count))
    ]
    return pl.pallas_call(
        functools.partial(spread_kernel, spans),
        out_shape=jax.ShapeDtypeStruct(coeffs.shape, jnp.bfloat16),
        in_specs=[far] * 4,
        out_specs=pl.BlockSpec(memory_space=pltpu.VMEM),
        scratch_shapes=[
            pltpu.VMEM(reflection.shape, jnp.float32),
            pltpu.VMEM(interp.shape, jnp.float32),
            pltpu.VMEM((1, coef_count), jnp.int32),
            pltpu.VMEM((chunks, places, 2, 1, first, second, coef_count), jnp.bfloat16),
            pltpu.VMEM((chunks, places, 2, 1, first, second, coef_count), jnp.bfloat16),
            pltpu.VMEM(reflection.shape, jnp.bfloat16),
            pltpu.VMEM((2, spans[1], spans[0], first, second, coef_count), jnp.bfloat16),
            pltpu.VMEM((coef_count // lanes, 2 * box_count, lanes), jnp.float32),
            pltpu.VMEM((3, 8 * level_count * order_count, coef_count), jnp.float32),
            pltpu.VMEM((2 * level_count, 2, box_count, coef_count), jnp.float32),
            pltpu.VMEM((1, 2, box_count, coef_count), jnp.float32),
            pltpu.VMEM((2 * level_count, 2 * coef_count, 2 * coef_count), jnp.bfloat16),
            pltpu.SemaphoreType.DMA((3,)),
            pltpu.SemaphoreType.DMA((chunks, places)),
            pltpu.SemaphoreType.DMA((chunks,)),
            pltpu.SemaphoreType.DMA((chunks, places)),
            pltpu.SemaphoreType.DMA((chunks, places)),
            pltpu.SemaphoreType.DMA((spans[0],)),
            pltpu.SemaphoreType.DMA((spans[0],)),
            pltpu.SemaphoreType.DMA((spans[0], 2 * spans[1])),
            pltpu.SemaphoreType.DMA((spans[0], 2 * spans[1])),
        ],
        compiler_params=pltpu.CompilerParams(
            collective_id=0, has_side_effects=True, vmem_limit_bytes=40 * 2**20
        ),
        name="butterfly",
    )(*operands)


def on_device(coeffs, reflection, interp, orders):
    level_count = interp.shape[1]
    _, ills, first, second, _ = coeffs.shape
    spans = (lax.axis_size("src"), lax.axis_size("tgt"))
    covers = spans[0] * first == 2**level_count and spans[1] * second == 2**level_count
    if covers and ills % (spans[0] * spans[1]) == 0 and lax.axis_size("ill") == 2:
        return by_spreading(coeffs, reflection, interp, orders)
    return by_swaps(coeffs, reflection, interp, orders)


def solution(mesh):
    in_specs = (
        P(None, ("groups", "ill"), "src", "tgt", None),
        P(None, ("groups", "src"), "tgt", None),
        P(),
        P(),
    )
    out_specs = P(None, ("groups", "ill"), "src", "tgt", None)
    return jax.shard_map(
        on_device, mesh=mesh, in_specs=in_specs, out_specs=out_specs, check_vma=False
    )
```
